512 devices in a mesh: blk: 32 (over z, y_lo), sub: 16 (over x, y_hi, core).
Axes of the slice: x: 4, y: 4 (y_hi: 2, y_lo: 2; y = y_hi * 2 + y_lo), z: 16, core: 2. Of those that a mesh axis runs over, the one named last changes fastest.
Arguments:
- rhs_interior: bfloat16 [4096, 16, 2, 128], P(('blk', 'sub')), may hold values from -6 to 6
- block_inverse: bfloat16 [4096, 2, 128, 128], P(('blk', 'sub')), may hold values from -0.5 to 0.5
- rhs_interface: float32 [16, 262144], P(None, ('blk', 'sub')), may hold values from -6 to 6
- band_cells: int32 [5, 262144], P(None, ('blk', 'sub')), may hold values from 0 to 255
- band_weights: float32 [5, 262144], P(None, ('blk', 'sub')), may hold values from -4 to 4
- group_map: int32 [32, 8192], P('blk'), may hold values from 0 to 4095, as said below
- schur_slab: float32 [2048, 131072], P('blk', 'sub'), may hold values from -0.03125 to 0.03125
Outputs:
- interior_update: float32 [4096, 16, 2, 128], P(('blk', 'sub'))
- slab_residual: float32 [16, 2048], P(None, ('blk', 'sub'))
The draws below stay inside these ranges and needn't reach their ends.
Inputs may be any that keep to these rules, and one draw needn't show every extreme that they name: `group_map`: within a row block, the rows of each device name each owner index exactly 512 / 16 times, and every assembled unknown of the block is named by exactly two rows.
All inputs are finite; a program needn't handle non-finite values.
Results may differ from the reference program's by a relative error of at most 0.0028.
Values sent between devices are 32-bit elements; how exact they have to be, the bound alone decides.
No kernel may reach another device: no remote copies, remote signals or barrier semaphores. Data moves between devices by JAX's collectives and lax.ppermute only.
A program may use at most 64 MiB of HBM per device.

```python
import jax
import jax.numpy as jnp
from jax import lax

SPECIES = 16
BLOCKS = 2
BLOCK_CELLS = 128
FACE_ROWS = 64
COUPLED = 5
ROWS_DEV = 4
CELLS = 256
LOCAL_ROWS = 512
SLOTS = 256
CYCLE = 32
SPREAD = 16
SUBDOMAINS = 4096
ALL_ROWS = 262144
ORDER = 131072
SLAB = 2048


def one_group(group_key):
    first_key, second_key = jax.random.split(group_key)
    per_peer = LOCAL_ROWS // SPREAD
    base_targets = jnp.repeat(jnp.arange(SPREAD, dtype=jnp.int32), per_peer)
    target_keys = jax.random.split(first_key, SPREAD)
    target = jax.vmap(lambda single: jax.random.permutation(single, base_targets))(target_keys)
    onehot = (target[:, :, None] == jnp.arange(SPREAD, dtype=jnp.int32)[None, None, :]).astype(jnp.int32)
    rank_in = jnp.sum(onehot * (jnp.cumsum(onehot, axis=1) - 1), axis=2)
    arrival = jnp.arange(SPREAD, dtype=jnp.int32)[:, None] * per_peer + rank_in
    base_slots = jnp.repeat(jnp.arange(SLOTS, dtype=jnp.int32), 2)
    slot_keys = jax.random.split(second_key, SPREAD)
    slot_perms = jax.vmap(lambda single: jax.random.permutation(single, base_slots))(slot_keys)
    placed = slot_perms[target, arrival]
    return (target * SLOTS + placed).reshape(-1)


def draw_group_map(key, part):
    group_keys = jax.random.split(jax.random.fold_in(key, 7), CYCLE)
    return jax.vmap(one_group)(group_keys).astype(jnp.int32)


def plant(array, stream_key, smallest, largest):
    longest = array.shape.index(max(array.shape))
    spots = []
    for shift in (0, 1):
        where = [jax.random.randint(jax.random.fold_in(stream_key, axis), (), 0, length) for axis, length in enumerate(array.shape)]
        where[longest] = (where[longest] + shift) % array.shape[longest]
        spots.append(tuple(where))
    return array.at[spots[0]].set(smallest).at[spots[1]].set(largest)


def raised(entries, stream_key, source, target, parts, factor):
    owner, partner = [(jnp.arange(entries.shape[axis_at]) // (entries.shape[axis_at] // parts)).reshape([-1 if axis == axis_at else 1 for axis in range(entries.ndim)]) for axis_at in (source, target)]
    chosen = jax.random.permutation(stream_key, parts)[partner]
    strong = (owner == chosen) | (owner == (partner + parts // 2) % parts)
    return jnp.where(strong, factor * entries, entries)


def steps_of(rng, shape, pieces, smallest, top_value):
    def one(axis_at, shards_of):
        heights = jax.random.uniform(jax.random.fold_in(jax.random.fold_in(rng, 6), axis_at), (shards_of,), jnp.float32, smallest / len(pieces), top_value / len(pieces))
        return jnp.repeat(jnp.exp(heights), shape[axis_at] // shards_of).reshape((-1,) + (1,) * (len(shape) - axis_at - 1))

    factor_of = one(*pieces[0])
    for cut in pieces[1:]:
        factor_of = factor_of * one(*cut)
    return factor_of


def scatter_about(own_key, shape, spread, most, pieces=(), kind=jnp.bfloat16):
    gain = steps_of(own_key, shape, pieces, -0.22, 0.18) if pieces else 1.0
    result = jax.random.normal(own_key, shape, jnp.float32) * spread * gain
    return jnp.minimum(jnp.maximum(result, -most), most).astype(kind)


def heavy_noise(own_key, extent, spread, most, cuts, heavy, kind=jnp.bfloat16):
    result = spread * jax.random.normal(own_key, extent, jnp.float32)
    if cuts:
        result = result * steps_of(own_key, extent, cuts, -0.22, 0.18)
    return jnp.clip(raised(result, jax.random.fold_in(own_key, 3), *heavy), -most, most).astype(kind)


def setup_inputs(seed: int = 0) -> dict:
    streams_of = jax.random.split(jax.random.key(seed), 8)
    return {
        "rhs_interior": scatter_about(streams_of[0], (SUBDOMAINS, SPECIES, BLOCKS, BLOCK_CELLS), 1.0, 6.0, ((0, 512),)),
        "block_inverse": scatter_about(streams_of[1], (SUBDOMAINS, BLOCKS, BLOCK_CELLS, BLOCK_CELLS), BLOCK_CELLS ** -0.5, 0.5, ((0, 512),)),
        "rhs_interface": scatter_about(streams_of[2], (SPECIES, ALL_ROWS), 1.0, 6.0, ((1, 512),), jnp.float32),
        "band_cells": plant(jax.random.randint(streams_of[3], (COUPLED, ALL_ROWS), 0, CELLS), jax.random.fold_in(streams_of[3], 1), 0, CELLS - 1).astype(jnp.int32),
        "band_weights": scatter_about(streams_of[4], (COUPLED, ALL_ROWS), 0.6, 4.0, ((1, 512),), jnp.float32),
        "group_map": draw_group_map(jax.random.fold_in(streams_of[7], 71), 0),
        "schur_slab": heavy_noise(streams_of[6], (SLAB, ORDER), ORDER ** -0.5, 0.03125, ((0, 32), (1, 16)), (1, 0, 32, 2.75), jnp.float32),
    }


def apply_blocks(values, inverses):
    return jnp.einsum('dsbk,dbjk->dsbj', values.astype(jnp.float32), inverses.astype(jnp.float32))


def reference(rhs_interior, block_inverse, rhs_interface, band_cells, band_weights, group_map, schur_slab):
    interior = apply_blocks(rhs_interior, block_inverse)
    flat_cells = jnp.transpose(interior.reshape(SUBDOMAINS, SPECIES, CELLS), (1, 0, 2)).reshape(SPECIES, SUBDOMAINS * CELLS)
    row_ids = jnp.arange(ALL_ROWS, dtype=jnp.int32)
    cell_index = (row_ids // FACE_ROWS)[None, :] * CELLS + band_cells
    picked = flat_cells[:, cell_index]
    face_values = rhs_interface - jnp.sum(band_weights[None] * picked, axis=1)
    block_of = row_ids // (SPREAD * LOCAL_ROWS)
    mapped = group_map.reshape(-1)
    column = ((mapped // SLOTS) * CYCLE + block_of) * SLOTS + mapped % SLOTS
    assembled = jnp.zeros((SPECIES, ORDER), jnp.float32).at[:, column].add(face_values)
    product = lax.dot_general(assembled, schur_slab, (((1,), (1,)), ((), ())), precision=lax.Precision.HIGHEST, preferred_element_type=jnp.float32)
    slab_ids = jnp.arange(SLAB, dtype=jnp.int32)
    slab_block = slab_ids // (SPREAD * ROWS_DEV)
    slab_owner = (slab_ids // ROWS_DEV) % SPREAD
    slab_column = (slab_owner * CYCLE + slab_block) * SLOTS + slab_ids % ROWS_DEV
    slab_residual = assembled[:, slab_column] - product
    row_values = assembled[:, column]
    contrib = (band_weights[None] * row_values[:, None, :]).reshape(SPECIES, COUPLED * ALL_ROWS)
    correction = jnp.zeros((SPECIES, SUBDOMAINS * CELLS), jnp.float32).at[:, cell_index.reshape(-1)].add(contrib)
    correction = jnp.transpose(correction.reshape(SPECIES, SUBDOMAINS, BLOCKS, BLOCK_CELLS), (1, 0, 2, 3))
    reduced = (rhs_interior.astype(jnp.float32) - correction).astype(jnp.bfloat16)
    interior_update = apply_blocks(reduced, block_inverse)
    return interior_update, slab_residual
```

```python
import functools

import jax
import jax.numpy as jnp
from jax import lax
from jax.experimental import pallas as pl
from jax.experimental.pallas import tpu as pltpu
from jax.sharding import Mesh
from jax.sharding import PartitionSpec as P

F32, BF16, I32 = jnp.float32, jnp.bfloat16, jnp.int32
NN = (((1,), (0,)), ((), ()))
NT = (((1,), (1,)), ((), ()))
SUB = ("x", "yh", "c")


def mxu(a, b, dims=NN):
    return lax.dot_general(a, b, dims, preferred_element_type=F32)


def halves(x):
    hi = x.astype(BF16)
    return hi, (x - hi.astype(F32)).astype(BF16)


def thirds(x):
    hi = x.astype(BF16)
    rest = x - hi.astype(F32)
    mid = rest.astype(BF16)
    return hi, mid, (rest - mid.astype(F32)).astype(BF16)


def iota(shape, axis):
    return lax.broadcasted_iota(I32, shape, axis)


def select_rows(x, onehot, dims):
    n = x.shape[0]
    y = mxu(jnp.concatenate(thirds(x), axis=0), onehot, dims)
    return y[:n] + y[n : 2 * n] + y[2 * n :]


def before(n):
    return (iota((n, n), 0) < iota((n, n), 1)).astype(F32).astype(BF16)


def pack(x, store):
    lane = iota((4, 128), 1) // 32
    for u in range(x.shape[1] // 128):
        tile = x[:, u * 128 : (u + 1) * 128]
        turned = [tile] + [pltpu.roll(tile, k * 32, 1) for k in range(1, 4)]
        for v in range(4):
            block = turned[(0 - v) % 4][0:4]
            for b in range(1, 4):
                block = jnp.where(lane == b, turned[(b - v) % 4][4 * b : 4 * b + 4], block)
            store(4 * u + v, block)


def unpack(load, peers):
    lane = iota((4, 128), 1) // 32
    tiles = []
    for u in range(peers // 4):
        blocks = [load(4 * u + v) for v in range(4)]
        turned = [[blk] + [pltpu.roll(blk, k * 32, 1) for k in range(1, 4)] for blk in blocks]
        rows = []
        for b in range(4):
            part = turned[0][(0 - b) % 4]
            for v in range(1, 4):
                part = jnp.where(lane == v, turned[v][(v - b) % 4], part)
            rows.append(part)
        tiles.append(jnp.concatenate(rows, axis=0))
    return jnp.concatenate(tiles, axis=1)


def send_order(map_ref, own, rows, peers, slots):
    target = map_ref[:, pl.ds(pl.multiple_of(own * rows, 128), rows)] // slots
    hit = iota((peers, rows), 0) == target
    ahead = mxu(hit.astype(F32).astype(BF16), before(rows))
    rank = jnp.sum(jnp.where(hit, ahead, 0.0), axis=0, keepdims=True).astype(I32)
    place = target * (rows // peers) + rank
    return (iota((rows, rows), 0) == place).astype(F32).astype(BF16)


def coupling(cells_ref, weights_ref, cells):
    coupled, rows = cells_ref.shape
    cell = iota((cells, rows), 0)
    total = jnp.zeros((cells, rows), F32)
    for c in range(coupled):
        total += jnp.where(cell == cells_ref[c : c + 1, :], weights_ref[c : c + 1, :], 0.0)
    return total


def solve(x, inv_ref, d):
    odd = iota((x.shape[0], 128), 0) % 2 == 1
    return jnp.where(odd, mxu(x, inv_ref[d, 1], NT), mxu(x, inv_ref[d, 0], NT))


def front_kernel(
    own_ref, map_ref, cells_ref, weights_ref, face_ref, rhs_ref, inv_ref, out_ref, sums
):
    subs, twice = rhs_ref.shape[0], rhs_ref.shape[1]
    rows = face_ref.shape[1]
    peers = out_ref.shape[0]
    order = send_order(map_ref, own_ref[0], rows, peers, rows // 2)
    whi, wlo = halves(coupling(cells_ref, weights_ref, 256))
    odd = iota((twice, 128), 0) % 2 == 1
    lane = iota((twice, 128), 1)
    for t in range(subs // 2):
        parts = []
        for d in (2 * t, 2 * t + 1):
            y = solve(rhs_ref[d], inv_ref, d)
            parts.append(
                jnp.concatenate([jnp.where(odd, 0.0, y), jnp.where(odd, y, 0.0)], axis=1)
            )
        hi, lo = halves(jnp.concatenate(parts, axis=0))
        cols = slice(t * 128, (t + 1) * 128)
        z = mxu(jnp.concatenate([hi, lo], axis=0), whi[:, cols])
        z = z[: 2 * twice] + z[2 * twice :] + mxu(hi, wlo[:, cols])
        sums[t] = jnp.where(lane < 64, z[:twice], z[twice:])
    half = twice // 2
    faces = [
        face_ref[:, t * 128 : (t + 1) * 128]
        - (sums[t, pl.ds(0, half, stride=2), :] + sums[t, pl.ds(1, half, stride=2), :])
        for t in range(subs // 2)
    ]
    outgoing = select_rows(jnp.concatenate(faces, axis=1), order, NT)

    def store(t, block):
        out_ref[t] = block

    pack(outgoing, store)


def landing_kernel(own_ref, map_ref, out_ref, targets, slots_of):
    peers = targets.shape[0]
    rows, slots = out_ref.shape
    for p in range(peers):
        targets[p : p + 1, :] = map_ref[:, p * rows : (p + 1) * rows]
    hit = targets[...] // slots == own_ref[0]
    ahead = mxu(hit.astype(F32).astype(BF16), before(rows)).astype(I32)
    key = jnp.where(hit, ahead, -1)
    slot = (targets[...] % slots).astype(F32)
    per = rows // peers
    for p in range(peers):
        mine = iota((per, rows), 0) == key[p : p + 1, :]
        slots_of[p * per : (p + 1) * per, :] = jnp.sum(
            jnp.where(mine, slot[p : p + 1, :], 0.0), axis=1, keepdims=True
        )
    column = slots_of[...].astype(I32)
    out_ref[...] = (iota((rows, slots), 1) == column).astype(F32).astype(BF16)


def assemble_kernel(in_ref, landing_ref, out_ref):
    incoming = unpack(lambda t: in_ref[t], in_ref.shape[0])
    out_ref[...] = select_rows(incoming, landing_ref[...], NN)


def return_kernel(panel_ref, landing_ref, out_ref):
    def store(t, block):
        out_ref[t] = block

    pack(select_rows(panel_ref[...], landing_ref[...], NT), store)


def product_kernel(own_ref, panels_ref, slab_ref, other_ref, out_ref):
    count, species, slots = panels_ref.shape
    rows = slab_ref.shape[0]
    y = own_ref[0]
    total = jnp.zeros((2 * rows, 2 * species), F32)
    low = jnp.zeros((2 * rows, species), F32)
    for z in range(count):
        mine = slab_ref[:, pl.ds(pl.multiple_of((2 * z + y) * slots, 128), slots)]
        both = jnp.concatenate([mine, other_ref[:, z * slots : (z + 1) * slots]], axis=0)
        shi, slo = halves(both)
        phi, plo = halves(panels_ref[z])
        total += mxu(shi, jnp.concatenate([phi, plo], axis=0), NT)
        low += mxu(slo, phi, NT)
    result = total[:, :species] + total[:, species:] + low
    result = jnp.concatenate([result, jnp.zeros((2 * rows, 128 - species), F32)], axis=1)
    out_ref[pl.ds(pl.multiple_of(y * rows, 8), rows), :] = result[:rows]
    out_ref[pl.ds(pl.multiple_of((1 - y) * rows, 8), rows), :] = result[rows:]


def residual_kernel(in_ref, panel_ref, out_ref):
    total = jnp.sum(in_ref[...], axis=0)
    species = panel_ref.shape[0]
    eye = (iota((species, 128), 0) == iota((species, 128), 1)).astype(F32)
    rows = lax.dot_general(eye, total, NT, precision=lax.Precision.HIGHEST, preferred_element_type=F32)
    out_ref[...] = panel_ref[:, : rows.shape[1]] - rows


def back_kernel(
    own_ref, map_ref, cells_ref, weights_ref, in_ref, rhs_ref, inv_ref, out_ref, twofold
):
    subs, twice = rhs_ref.shape[0], rhs_ref.shape[1]
    rows = cells_ref.shape[1]
    peers = in_ref.shape[0]
    order = send_order(map_ref, own_ref[0], rows, peers, rows // 2)
    whi, wlo = halves(coupling(cells_ref, weights_ref, 256))
    values = select_rows(unpack(lambda t: in_ref[t], peers), order, NN)
    half = twice // 2
    for t in range(subs // 2):
        twofold[t, pl.ds(0, half, stride=2), :] = values[:, t * 128 : (t + 1) * 128]
        twofold[t, pl.ds(1, half, stride=2), :] = values[:, t * 128 : (t + 1) * 128]
    odd = iota((twice, 128), 0) % 2 == 1
    lane = iota((twice, 128), 1)
    for t in range(subs // 2):
        cols = slice(t * 128, (t + 1) * 128)
        v = twofold[t]
        hi, lo = halves(jnp.concatenate([jnp.where(lane < 64, v, 0.0), jnp.where(lane < 64, 0.0, v)], axis=0))
        z = mxu(jnp.concatenate([hi, lo], axis=0), whi[:, cols], NT)
        z = z[: 2 * twice] + z[2 * twice :] + mxu(hi, wlo[:, cols], NT)
        for i, d in enumerate((2 * t, 2 * t + 1)):
            part = z[i * twice : (i + 1) * twice]
            correction = jnp.where(odd, part[:, 128:], part[:, :128])
            reduced = (rhs_ref[d].astype(F32) - correction).astype(BF16)
            out_ref[d] = solve(reduced, inv_ref, d)


SMEM = pl.BlockSpec(memory_space=pltpu.SMEM)
VMEM = pl.BlockSpec(memory_space=pltpu.VMEM)


def call(kernel, name, shape, *args, dtype=F32, scratch=()):
    specs = [SMEM if a.ndim == 1 else VMEM for a in args]
    return pl.pallas_call(
        kernel,
        out_shape=jax.ShapeDtypeStruct(shape, dtype),
        in_specs=specs,
        out_specs=VMEM,
        scratch_shapes=scratch,
        name=name,
    )(*args)


def per_device(rhs, inverse, rhs_face, cells, weights, group_map, slab):
    subs, species, blocks, width = rhs.shape
    rows = rhs_face.shape[1]
    slots = rows // 2
    peers = lax.axis_size(SUB)
    levels = lax.axis_size("z")
    slab_rows = slab.shape[0]
    own = lax.axis_index(SUB).astype(I32).reshape(1)
    side = lax.axis_index("yl").astype(I32).reshape(1)
    rhs2 = rhs.reshape(subs, species * blocks, width)

    outgoing = call(
        front_kernel, "front", (peers, 4, 128), own, group_map, cells, weights, rhs_face, rhs2,
        inverse, scratch=[pltpu.VMEM((subs // 2, species * blocks, 128), F32)],
    )
    incoming = lax.all_to_all(outgoing, SUB, 0, 0)
    paired = slab.reshape(slab_rows, levels, 2, slots)
    away = jnp.where(side[0] == 0, paired[:, :, 1], paired[:, :, 0]).reshape(slab_rows, levels * slots)
    other = lax.ppermute(away, "yl", [(0, 1), (1, 0)])
    landing = call(
        landing_kernel, "landing", (rows, slots), own, group_map, dtype=BF16,
        scratch=[pltpu.VMEM((peers, rows), I32), pltpu.VMEM((rows, 1), F32)],
    )
    panel = call(assemble_kernel, "assemble", (species, slots), incoming, landing)
    panels = lax.all_to_all(jnp.broadcast_to(panel[None], (levels, species, slots)), "z", 0, 0)
    returning = call(return_kernel, "giveback", (peers, 4, 128), panel, landing)
    returned = lax.all_to_all(returning, SUB, 0, 0)
    update = call(
        back_kernel, "back", (subs, species * blocks, width), own, group_map, cells, weights,
        returned, rhs2, inverse, scratch=[pltpu.VMEM((subs // 2, species * blocks, 128), F32)],
    )
    partial = call(product_kernel, "product", (2 * slab_rows, 128), side, panels, slab, other)
    partial = partial.reshape(2 * peers, slab_rows // peers, 128)
    shares = lax.all_to_all(partial, ("yl",) + SUB, 0, 0)
    residual = call(residual_kernel, "residual", (species, slab_rows // peers), shares, panel)
    return update.reshape(rhs.shape), residual


def solution(mesh):
    fine = Mesh(mesh.devices.reshape(16, 2, 4, 2, 2), ("z", "yl", "x", "yh", "c"))
    blk, sub = ("z", "yl"), SUB
    every = blk + sub
    placed = (
        P(every, None, None, None),
        P(every, None, None, None),
        P(None, every),
        P(None, every),
        P(None, every),
        P(blk, None),
        P(blk, sub),
    )
    return jax.shard_map(
        per_device,
        mesh=fine,
        in_specs=placed,
        out_specs=(P(every, None, None, None), P(None, every)),
        check_vma=False,
    )
```

```python
import functools

import jax
import jax.numpy as jnp
from jax import lax
from jax.experimental import pallas as pl
from jax.experimental.pallas import tpu as pltpu
from jax.sharding import Mesh
from jax.sharding import PartitionSpec as P

F32, BF16, I32 = jnp.float32, jnp.bfloat16, jnp.int32
NN = (((1,), (0,)), ((), ()))
NT = (((1,), (1,)), ((), ()))
SUB = ("x", "yh", "c")


def mxu(a, b, dims=NN):
    return lax.dot_general(a, b, dims, preferred_element_type=F32)


def halves(x):
    hi = x.astype(BF16)
    return hi, (x - hi.astype(F32)).astype(BF16)


def thirds(x):
    hi = x.astype(BF16)
    rest = x - hi.astype(F32)
    mid = rest.astype(BF16)
    return hi, mid, (rest - mid.astype(F32)).astype(BF16)


def iota(shape, axis):
    return lax.broadcasted_iota(I32, shape, axis)


def select_rows(x, onehot, dims):
    n = x.shape[0]
    y = mxu(jnp.concatenate(thirds(x), axis=0), onehot, dims)
    return y[:n] + y[n : 2 * n] + y[2 * n :]


def before(n):
    return (iota((n, n), 0) < iota((n, n), 1)).astype(F32).astype(BF16)


def pack(x, store):
    lane = iota((4, 128), 1) // 32
    for u in range(x.shape[1] // 128):
        tile = x[:, u * 128 : (u + 1) * 128]
        turned = [tile] + [pltpu.roll(tile, k * 32, 1) for k in range(1, 4)]
        for v in range(4):
            block = turned[(0 - v) % 4][0:4]
            for b in range(1, 4):
                block = jnp.where(lane == b, turned[(b - v) % 4][4 * b : 4 * b + 4], block)
            store(4 * u + v, block)


def unpack(load, peers):
    lane = iota((4, 128), 1) // 32
    tiles = []
    for u in range(peers // 4):
        blocks = [load(4 * u + v) for v in range(4)]
        turned = [[blk] + [pltpu.roll(blk, k * 32, 1) for k in range(1, 4)] for blk in blocks]
        rows = []
        for b in range(4):
            part = turned[0][(0 - b) % 4]
            for v in range(1, 4):
                part = jnp.where(lane == v, turned[v][(v - b) % 4], part)
            rows.append(part)
        tiles.append(jnp.concatenate(rows, axis=0))
    return jnp.concatenate(tiles, axis=1)


def send_order(mapped, peers, slots):
    rows = mapped.shape[1]
    target = mapped // slots
    hit = iota((peers, rows), 0) == target
    ahead = mxu(hit.astype(F32).astype(BF16), before(rows))
    rank = jnp.sum(jnp.where(hit, ahead, 0.0), axis=0, keepdims=True).astype(I32)
    place = target * (rows // peers) + rank
    return (iota((rows, rows), 0) == place).astype(F32).astype(BF16)


def coupling(cells_ref, weights_ref, cells):
    coupled, rows = cells_ref.shape
    cell = iota((cells, rows), 0)
    total = jnp.zeros((cells, rows), F32)
    for c in range(coupled):
        total += jnp.where(cell == cells_ref[c : c + 1, :], weights_ref[c : c + 1, :], 0.0)
    return total


def solve(x, inv_ref, d):
    odd = iota((x.shape[0], 128), 0) % 2 == 1
    return jnp.where(odd, mxu(x, inv_ref[d, 1], NT), mxu(x, inv_ref[d, 0], NT))


def front_kernel(
    own_ref, map_hbm, cells_hbm, weights_hbm, face_hbm, rhs_hbm, inv_hbm,
    out_ref, order_ref, whi_ref, wlo_ref,
    sums, map_ref, cells_ref, weights_ref, face_ref, rhs_ref, inv_ref, sems,
):
    subs, twice = rhs_ref.shape[0], rhs_ref.shape[1]
    rows = face_ref.shape[1]
    peers = out_ref.shape[0]
    here = pl.ds(pl.multiple_of(own_ref[0] * rows, 128), rows)
    copies = [
        pltpu.make_async_copy(source, target, sems.at[i])
        for i, (source, target) in enumerate(
            (
                (map_hbm.at[:, here], map_ref),
                (cells_hbm, cells_ref),
                (weights_hbm, weights_ref),
                (face_hbm, face_ref),
                (rhs_hbm, rhs_ref),
                (inv_hbm, inv_ref),
            )
        )
    ]
    for copy in copies:
        copy.start()
    for copy in copies[:3]:
        copy.wait()
    order = send_order(map_ref[...], peers, rows // 2)
    whi, wlo = halves(coupling(cells_ref, weights_ref, whi_ref.shape[0]))
    order_ref[...], whi_ref[...], wlo_ref[...] = order, whi, wlo
    for copy in copies[3:]:
        copy.wait()
    odd = iota((twice, 128), 0) % 2 == 1
    lane = iota((twice, 128), 1)
    for t in range(subs // 2):
        parts = []
        for d in (2 * t, 2 * t + 1):
            y = solve(rhs_ref[d], inv_ref, d)
            parts.append(
                jnp.concatenate([jnp.where(odd, 0.0, y), jnp.where(odd, y, 0.0)], axis=1)
            )
        hi, lo = halves(jnp.concatenate(parts, axis=0))
        cols = slice(t * 128, (t + 1) * 128)
        z = mxu(jnp.concatenate([hi, lo], axis=0), whi[:, cols])
        z = z[: 2 * twice] + z[2 * twice :] + mxu(hi, wlo[:, cols])
        sums[t] = jnp.where(lane < 64, z[:twice], z[twice:])
    half = twice // 2
    faces = [
        face_ref[:, t * 128 : (t + 1) * 128]
        - (sums[t, pl.ds(0, half, stride=2), :] + sums[t, pl.ds(1, half, stride=2), :])
        for t in range(subs // 2)
    ]
    outgoing = select_rows(jnp.concatenate(faces, axis=1), order, NT)

    def store(t, block):
        out_ref[t] = block

    pack(outgoing, store)


def landing_kernel(own_ref, map_ref, out_ref, targets, slots_of):
    peers = targets.shape[0]
    rows, slots = out_ref.shape
    for p in range(peers):
        targets[p : p + 1, :] = map_ref[:, p * rows : (p + 1) * rows]
    hit = targets[...] // slots == own_ref[0]
    ahead = mxu(hit.astype(F32).astype(BF16), before(rows)).astype(I32)
    key = jnp.where(hit, ahead, -1)
    slot = (targets[...] % slots).astype(F32)
    per = rows // peers
    for p in range(peers):
        mine = iota((per, rows), 0) == key[p : p + 1, :]
        slots_of[p * per : (p + 1) * per, :] = jnp.sum(
            jnp.where(mine, slot[p : p + 1, :], 0.0), axis=1, keepdims=True
        )
    column = slots_of[...].astype(I32)
    out_ref[...] = (iota((rows, slots), 1) == column).astype(F32).astype(BF16)


def column_of(j, side):
    if POOL == "yl":
        return 2 * j + side
    return 4 * (j // 2) + 2 * side + j % 2


def cut_kernel(side_ref, slab_ref, away_ref, hi_ref, lo_ref, mine, sems):
    slots = SLOTS
    count = away_ref.shape[1] // slots
    side = side_ref[0]
    copies = []
    for j in range(count):
        here = pl.ds(j * slots, slots)
        for i, (member, target) in enumerate(((1 - side, away_ref), (side, mine))):
            there = pl.ds(pl.multiple_of(column_of(j, member) * slots, 128), slots)
            copy = pltpu.make_async_copy(
                slab_ref.at[:, there], target.at[:, here], sems.at[i, j]
            )
            copy.start()
            copies.append(copy)
    for copy in copies:
        copy.wait()
    hi, lo = halves(mine[...])
    hi_ref[...], lo_ref[...] = hi, lo


def assemble_kernel(in_ref, landing_ref, out_ref):
    incoming = unpack(lambda t: in_ref[t], in_ref.shape[0])
    out_ref[...] = select_rows(incoming, landing_ref[...], NN)


def product_kernel(
    side_ref, panels_ref, hi_ref, lo_ref, other_ref, panel_ref, landing_ref, out_ref
):
    count, species, slots = panels_ref.shape
    rows = hi_ref.shape[0]
    peers = out_ref.shape[0] // 2
    side = side_ref[0]
    total = jnp.zeros((2 * rows, 2 * species), F32)
    low = jnp.zeros((2 * rows, species), F32)
    for j in range(count):
        cols = slice(j * slots, (j + 1) * slots)
        ohi, olo = halves(other_ref[:, cols])
        phi, plo = halves(panels_ref[j])
        shi = jnp.concatenate([hi_ref[:, cols], ohi], axis=0)
        slo = jnp.concatenate([lo_ref[:, cols], olo], axis=0)
        total += mxu(shi, jnp.concatenate([phi, plo], axis=0), NT)
        low += mxu(slo, phi, NT)
    result = total[:, :species] + total[:, species:] + low
    result = jnp.concatenate([result, jnp.zeros((2 * rows, 128 - species), F32)], axis=1)
    mine, other = side * peers, (1 - side) * peers
    per = rows // peers
    nothing = jnp.zeros((4, 128), F32)
    for p in range(peers):
        out_ref[mine + p, 0:per, :] = result[p * per : (p + 1) * per]
        out_ref[other + p, 0:per, :] = result[rows + p * per : rows + (p + 1) * per]
        out_ref[other + p, per : per + 4, :] = nothing

    def store(t, block):
        out_ref[mine + t, per : per + 4, :] = block

    pack(select_rows(panel_ref[...], landing_ref[...], NT), store)


def back_kernel(
    side_ref, in_ref, panel_ref, order_ref, whi_ref, wlo_ref, rhs_ref, inv_ref,
    out_ref, residual_ref, twofold,
):
    subs, twice = rhs_ref.shape[0], rhs_ref.shape[1]
    peers = in_ref.shape[0] // 2
    per, species = residual_ref.shape
    total = jnp.sum(in_ref[...], axis=0)
    eye = (iota((8, 128), 0) == iota((8, 128), 1)).astype(F32)
    first = lax.dot_general(
        eye, panel_ref[:, :128], NT, precision=lax.Precision.HIGHEST, preferred_element_type=F32
    )
    residual_ref[...] = (first - total[:, :species])[:per]
    mine = side_ref[0] * peers
    returned = unpack(lambda t: in_ref[mine + t, per : per + 4, :], peers)
    values = select_rows(returned, order_ref[...], NN)
    half = twice // 2
    for t in range(subs // 2):
        twofold[t, pl.ds(0, half, stride=2), :] = values[:, t * 128 : (t + 1) * 128]
        twofold[t, pl.ds(1, half, stride=2), :] = values[:, t * 128 : (t + 1) * 128]
    odd = iota((twice, 128), 0) % 2 == 1
    lane = iota((twice, 128), 1)
    for t in range(subs // 2):
        cols = slice(t * 128, (t + 1) * 128)
        v = twofold[t]
        hi, lo = halves(
            jnp.concatenate([jnp.where(lane < 64, v, 0.0), jnp.where(lane < 64, 0.0, v)], axis=0)
        )
        z = mxu(jnp.concatenate([hi, lo], axis=0), whi_ref[:, cols], NT)
        z = z[: 2 * twice] + z[2 * twice :] + mxu(hi, wlo_ref[:, cols], NT)
        for i, d in enumerate((2 * t, 2 * t + 1)):
            part = z[i * twice : (i + 1) * twice]
            correction = jnp.where(odd, part[:, 128:], part[:, :128])
            reduced = (rhs_ref[d].astype(F32) - correction).astype(BF16)
            out_ref[d] = solve(reduced, inv_ref, d)


POOL = "yl"
GATHER = ("zh", "zl") if POOL == "yl" else ("zh", "yl")
RING = False
SLOTS = 256
VMEM = pltpu.VMEM


def vm(x):
    return pltpu.with_memory_space_constraint(x, pltpu.VMEM)


def call(kernel, name, outs, *args, scratch=(), hbm=()):
    specs = [
        pl.BlockSpec(
            memory_space=pltpu.SMEM if a.ndim == 1 else pltpu.HBM if i in hbm else pltpu.VMEM
        )
        for i, a in enumerate(args)
    ]
    args = [
        pltpu.with_memory_space_constraint(a, pltpu.HBM) if i in hbm else a
        for i, a in enumerate(args)
    ]
    whole = pl.BlockSpec(memory_space=pltpu.VMEM)
    return pl.pallas_call(
        kernel,
        out_shape=outs,
        in_specs=specs,
        out_specs=[whole] * len(outs) if isinstance(outs, list) else whole,
        scratch_shapes=scratch,
        name=name,
        compiler_params=pltpu.CompilerParams(vmem_limit_bytes=16 << 20),
    )(*args)


def per_device(rhs, inverse, rhs_face, cells, weights, group_map, slab):
    subs, species, blocks, width = rhs.shape
    rows = rhs_face.shape[1]
    slots = rows // 2
    peers = lax.axis_size(SUB)
    levels = lax.axis_size(GATHER)
    slab_rows = slab.shape[0]
    own = lax.axis_index(SUB).astype(I32).reshape(1)
    side = lax.axis_index(POOL).astype(I32).reshape(1)
    rhs2 = rhs.reshape(subs, species * blocks, width)
    pairs = VMEM((subs // 2, species * blocks, 128), F32)

    outgoing, order, whi, wlo = call(
        front_kernel,
        "front",
        [
            VMEM((peers, 4, 128), F32),
            VMEM((rows, rows), BF16),
            VMEM((blocks * width, rows), BF16),
            VMEM((blocks * width, rows), BF16),
        ],
        own, group_map, cells, weights, rhs_face, rhs2, inverse,
        scratch=[pairs]
        + [
            VMEM(shape, kind)
            for shape, kind in (
                ((1, rows), I32),
                (cells.shape, I32),
                (weights.shape, F32),
                (rhs_face.shape, F32),
                (rhs2.shape, BF16),
                (inverse.shape, BF16),
            )
        ]
        + [pltpu.SemaphoreType.DMA((6,))],
        hbm=range(1, 7),
    )
    incoming = lax.all_to_all(outgoing, SUB, 0, 0)
    half = levels * slots
    away, hi, lo = call(
        cut_kernel,
        "cut",
        [VMEM((slab_rows, half), F32), VMEM((slab_rows, half), BF16), VMEM((slab_rows, half), BF16)],
        side, slab,
        scratch=[VMEM((slab_rows, half), F32), pltpu.SemaphoreType.DMA((2, levels))],
        hbm=(1,),
    )
    landing = call(
        landing_kernel, "landing", VMEM((rows, slots), BF16), own, group_map,
        scratch=[VMEM((peers, rows), I32), VMEM((rows, 1), F32)],
    )
    if POOL == "yl":
        incoming, away, landing = lax.optimization_barrier((incoming, away, landing))
    other = lax.ppermute(away, POOL, [(0, 1), (1, 0)])
    panel = call(
        assemble_kernel, "assemble", VMEM((species, slots), F32), vm(incoming), vm(landing)
    )
    if RING:
        panels = lax.all_gather(panel, GATHER, axis=0)
    else:
        panels = lax.all_to_all(jnp.broadcast_to(panel[None], (levels, species, slots)), GATHER, 0, 0)
    partial = call(
        product_kernel, "product", VMEM((2 * peers, 8, 128), F32),
        side, vm(panels), vm(hi), vm(lo), vm(other), vm(panel), vm(landing),
    )
    shares = lax.all_to_all(partial, (POOL,) + SUB, 0, 0)
    update, residual = call(
        back_kernel,
        "back",
        [
            jax.ShapeDtypeStruct((subs, species * blocks, width), F32),
            jax.ShapeDtypeStruct((slab_rows // peers, species), F32),
        ],
        side, vm(shares), vm(panel), vm(order), vm(whi), vm(wlo), rhs2, inverse,
        scratch=[pairs],
    )
    return update.reshape(rhs.shape), residual.T


def solution(mesh):
    fine = Mesh(mesh.devices.reshape(8, 2, 2, 4, 2, 2), ("zh", "zl", "yl", "x", "yh", "c"))
    blk, sub = ("zh", "zl", "yl"), SUB
    every = blk + sub
    placed = (
        P(every, None, None, None),
        P(every, None, None, None),
        P(None, every),
        P(None, every),
        P(None, every),
        P(blk, None),
        P(blk, sub),
    )
    return jax.shard_map(
        per_device,
        mesh=fine,
        in_specs=placed,
        out_specs=(P(every, None, None, None), P(None, every)),
        check_vma=False,
    )
```

```python
import jax
import jax.numpy as jnp
from jax import lax
from jax.experimental import pallas as pl
from jax.experimental.pallas import tpu as pltpu
from jax.sharding import Mesh
from jax.sharding import PartitionSpec as P

F32, BF16, I32 = jnp.float32, jnp.bfloat16, jnp.int32
NN = (((1,), (0,)), ((), ()))
NT = (((1,), (1,)), ((), ()))
SUB = ("x", "yh", "c")


def mxu(a, b, dims=NN):
    return lax.dot_general(a, b, dims, preferred_element_type=F32)


def halves(x):
    hi = x.astype(BF16)
    return hi, (x - hi.astype(F32)).astype(BF16)


def thirds(x):
    hi = x.astype(BF16)
    rest = x - hi.astype(F32)
    mid = rest.astype(BF16)
    return hi, mid, (rest - mid.astype(F32)).astype(BF16)


def iota(shape, axis):
    return lax.broadcasted_iota(I32, shape, axis)


def select_rows(x, onehot, dims):
    n = x.shape[0]
    y = mxu(jnp.concatenate(thirds(x), axis=0), onehot, dims)
    return y[:n] + y[n : 2 * n] + y[2 * n :]


def ranks(hit):
    n, rows = hit.shape
    hit = hit.astype(F32).astype(BF16)
    tiles = [hit[:, t : t + 128] for t in range(0, rows, 128)]
    row, col = iota((128, 256), 0), iota((128, 256), 1)
    ahead = ((row < col) | (col >= 128)).astype(F32).astype(BF16)
    counts = mxu(jnp.concatenate(tiles, axis=0), ahead)
    out, base = [], jnp.zeros((n, 128), F32)
    for t in range(len(tiles)):
        part = counts[t * n : (t + 1) * n]
        out.append(part[:, :128] + base)
        base = base + part[:, 128:]
    return jnp.concatenate(out, axis=1)


def row_numbers():
    return iota((256, 128), 0).astype(F32).astype(BF16)


def pack(x, store):
    lane = iota((4, 128), 1) // 32
    for u in range(x.shape[1] // 128):
        tile = x[:, u * 128 : (u + 1) * 128]
        turned = [tile] + [pltpu.roll(tile, k * 32, 1) for k in range(1, 4)]
        for v in range(4):
            block = turned[(0 - v) % 4][0:4]
            for b in range(1, 4):
                block = jnp.where(lane == b, turned[(b - v) % 4][4 * b : 4 * b + 4], block)
            store(4 * u + v, block)


def unpack(load, peers):
    lane = iota((4, 128), 1) // 32
    tiles = []
    for u in range(peers // 4):
        blocks = [load(4 * u + v) for v in range(4)]
        turned = [[blk] + [pltpu.roll(blk, k * 32, 1) for k in range(1, 4)] for blk in blocks]
        rows = []
        for b in range(4):
            part = turned[0][(0 - b) % 4]
            for v in range(1, 4):
                part = jnp.where(lane == v, turned[v][(v - b) % 4], part)
            rows.append(part)
        tiles.append(jnp.concatenate(rows, axis=0))
    return jnp.concatenate(tiles, axis=1)


def send_place(mapped, peers, slots):
    rows = mapped.shape[1]
    target = mapped // slots
    hit = iota((peers, rows), 0) == target
    rank = jnp.sum(jnp.where(hit, ranks(hit), 0.0), axis=0, keepdims=True)
    return target.astype(F32) * (rows // peers) + rank


def send_order(place, number, store):
    rows = place.shape[1]
    one, zero = jnp.ones((), BF16), jnp.zeros((), BF16)
    for h in range(0, rows, 256):
        inside = (place >= h) & (place < h + 256)
        local = jnp.where(inside, place - h, -1.0).astype(BF16)
        for t in range(0, rows, 128):
            store(h, t, jnp.where(number == local[:, t : t + 128], one, zero))


def coupling(cells, weights, number, store):
    coupled, rows = cells.shape
    cell = [cells[c : c + 1, :].astype(F32) for c in range(coupled)]
    weight = [weights[c : c + 1, :] for c in range(coupled)]
    for c in range(1, coupled):
        for e in range(c):
            same = cell[c] == cell[e]
            weight[e] = weight[e] + jnp.where(same, weight[c], 0.0)
            cell[c] = jnp.where(same, -1.0, cell[c])
    cell = [x.astype(BF16) for x in cell]
    parts = [halves(x) for x in weight]
    for t in range(0, rows, 128):
        high = low = jnp.zeros((256, 128), BF16)
        for c in range(coupled):
            here = number == cell[c][:, t : t + 128]
            high = jnp.where(here, parts[c][0][:, t : t + 128], high)
            low = jnp.where(here, parts[c][1][:, t : t + 128], low)
        store(t, high, low)


def solve(x, inv_ref, d):
    odd = iota((x.shape[0], 128), 0) % 2 == 1
    return jnp.where(odd, mxu(x, inv_ref[d, 1], NT), mxu(x, inv_ref[d, 0], NT))


def front_kernel(
    own_ref, side_ref, map_hbm, cells_hbm, weights_hbm, face_hbm, rhs_hbm, inv_hbm, slab_hbm,
    out_ref, place_ref, whi_ref, wlo_ref, map_ref, mine_ref, away_hbm,
    sums, order_ref, away_ref, cells_ref, weights_ref, face_ref, rhs_ref, inv_ref, sems, cuts,
):
    subs, twice = rhs_ref.shape[0], rhs_ref.shape[1]
    rows = face_ref.shape[1]
    peers = out_ref.shape[0]
    slots = rows // 2
    copies = [
        pltpu.make_async_copy(source, target, sems.at[i])
        for i, (source, target) in enumerate(
            (
                (map_hbm, map_ref),
                (cells_hbm, cells_ref),
                (weights_hbm, weights_ref),
                (face_hbm, face_ref),
                (rhs_hbm, rhs_ref),
                (inv_hbm, inv_ref),
            )
        )
    ]
    for copy in copies:
        copy.start()
    side = side_ref[0]
    slices = []
    for j in range(away_hbm.shape[1] // slots):
        here = pl.ds(j * slots, slots)
        for i, (member, target) in enumerate(((1 - side, away_ref), (side, mine_ref))):
            there = pl.ds(pl.multiple_of((2 * j + member) * slots, 128), slots)
            copy = pltpu.make_async_copy(slab_hbm.at[:, there], target.at[:, here], cuts.at[i, j])
            copy.start()
            slices.append(copy)
    number = row_numbers()
    for copy in copies[:3]:
        copy.wait()

    def order_block(h, t, block):
        order_ref[h : h + 256, t : t + 128] = block

    def coupling_block(t, high, low):
        whi_ref[:, t : t + 128] = high
        wlo_ref[:, t : t + 128] = low

    mapped = map_ref[:, pl.ds(pl.multiple_of(own_ref[0] * rows, 128), rows)]
    place = send_place(mapped, peers, slots)
    place_ref[...] = place
    send_order(place, number, order_block)
    for copy in slices[::2]:
        copy.wait()
    leaving = pltpu.make_async_copy(away_ref, away_hbm, sems.at[6])
    leaving.start()
    coupling(cells_ref[...], weights_ref[...], number, coupling_block)
    for copy in copies[3:]:
        copy.wait()
    for copy in slices[1::2]:
        copy.wait()
    odd = iota((twice, 128), 0) % 2 == 1
    lane = iota((twice, 128), 1)
    for t in range(subs // 2):
        parts = []
        for d in (2 * t, 2 * t + 1):
            y = solve(rhs_ref[d], inv_ref, d)
            parts.append(
                jnp.concatenate([jnp.where(odd, 0.0, y), jnp.where(odd, y, 0.0)], axis=1)
            )
        hi, lo = halves(jnp.concatenate(parts, axis=0))
        cols = slice(t * 128, (t + 1) * 128)
        z = mxu(jnp.concatenate([hi, lo], axis=0), whi_ref[:, cols])
        z = z[: 2 * twice] + z[2 * twice :] + mxu(hi, wlo_ref[:, cols])
        sums[t] = jnp.where(lane < 64, z[:twice], z[twice:])
    half = twice // 2
    faces = [
        face_ref[:, t * 128 : (t + 1) * 128]
        - (sums[t, pl.ds(0, half, stride=2), :] + sums[t, pl.ds(1, half, stride=2), :])
        for t in range(subs // 2)
    ]
    outgoing = select_rows(jnp.concatenate(faces, axis=1), order_ref[...], NT)

    def store(t, block):
        out_ref[t] = block

    pack(outgoing, store)
    leaving.wait()


def landing_kernel(own_ref, map_ref, out_ref, targets, slots_of):
    peers = targets.shape[0]
    rows, slots = out_ref.shape
    for p in range(peers):
        targets[p : p + 1, :] = map_ref[:, p * rows : (p + 1) * rows]
    hit = targets[...] // slots == own_ref[0]
    key = jnp.where(hit, ranks(hit).astype(I32), -1)
    slot = (targets[...] % slots).astype(F32)
    per = rows // peers
    for p in range(peers):
        mine = iota((per, rows), 0) == key[p : p + 1, :]
        slots_of[p * per : (p + 1) * per, :] = jnp.sum(
            jnp.where(mine, slot[p : p + 1, :], 0.0), axis=1, keepdims=True
        )
    column = slots_of[...].astype(I32)
    out_ref[...] = (iota((rows, slots), 1) == column).astype(F32).astype(BF16)


def assemble_kernel(in_ref, landing_ref, out_ref):
    incoming = unpack(lambda t: in_ref[t], in_ref.shape[0])
    out_ref[...] = select_rows(incoming, landing_ref[...], NN)


def product_kernel(
    side_ref, panels_ref, mine_ref, other_ref, panel_ref, landing_ref, out_ref
):
    count, species, slots = panels_ref.shape
    rows = mine_ref.shape[0]
    peers = out_ref.shape[0] // 2
    side = side_ref[0]
    total = jnp.zeros((2 * rows, 2 * species), F32)
    low = jnp.zeros((2 * rows, species), F32)
    for j in range(count):
        cols = slice(j * slots, (j + 1) * slots)
        shi, slo = halves(jnp.concatenate([mine_ref[:, cols], other_ref[:, cols]], axis=0))
        phi, plo = halves(panels_ref[j])
        total += mxu(shi, jnp.concatenate([phi, plo], axis=0), NT)
        low += mxu(slo, phi, NT)
    result = total[:, :species] + total[:, species:] + low
    result = jnp.concatenate([result, jnp.zeros((2 * rows, 128 - species), F32)], axis=1)
    mine, other = side * peers, (1 - side) * peers
    per = rows // peers
    nothing = jnp.zeros((4, 128), F32)
    for p in range(peers):
        out_ref[mine + p, 0:per, :] = result[p * per : (p + 1) * per]
        out_ref[other + p, 0:per, :] = result[rows + p * per : rows + (p + 1) * per]
        out_ref[other + p, per : per + 4, :] = nothing

    def store(t, block):
        out_ref[mine + t, per : per + 4, :] = block

    pack(select_rows(panel_ref[...], landing_ref[...], NT), store)


def back_kernel(
    side_ref, in_ref, panel_ref, place_ref, whi_ref, wlo_ref, rhs_ref, inv_ref,
    out_ref, residual_ref, twofold, order_ref,
):
    subs, twice = rhs_ref.shape[0], rhs_ref.shape[1]
    peers = in_ref.shape[0] // 2
    per, species = residual_ref.shape
    total = jnp.sum(in_ref[...], axis=0)
    eye = (iota((8, 128), 0) == iota((8, 128), 1)).astype(F32)
    first = lax.dot_general(
        eye, panel_ref[:, :128], NT, precision=lax.Precision.HIGHEST, preferred_element_type=F32
    )
    residual_ref[...] = (first - total[:, :species])[:per]
    mine = side_ref[0] * peers
    returned = unpack(lambda t: in_ref[mine + t, per : per + 4, :], peers)

    def order_block(h, t, block):
        order_ref[h : h + 256, t : t + 128] = block

    send_order(place_ref[...], row_numbers(), order_block)
    values = select_rows(returned, order_ref[...], NN)
    half = twice // 2
    for t in range(subs // 2):
        twofold[t, pl.ds(0, half, stride=2), :] = values[:, t * 128 : (t + 1) * 128]
        twofold[t, pl.ds(1, half, stride=2), :] = values[:, t * 128 : (t + 1) * 128]
    odd = iota((twice, 128), 0) % 2 == 1
    lane = iota((twice, 128), 1)
    for t in range(subs // 2):
        cols = slice(t * 128, (t + 1) * 128)
        v = twofold[t]
        hi, lo = halves(
            jnp.concatenate([jnp.where(lane < 64, v, 0.0), jnp.where(lane < 64, 0.0, v)], axis=0)
        )
        z = mxu(jnp.concatenate([hi, lo], axis=0), whi_ref[:, cols], NT)
        z = z[: 2 * twice] + z[2 * twice :] + mxu(hi, wlo_ref[:, cols], NT)
        for i, d in enumerate((2 * t, 2 * t + 1)):
            part = z[i * twice : (i + 1) * twice]
            correction = jnp.where(odd, part[:, 128:], part[:, :128])
            reduced = (rhs_ref[d].astype(F32) - correction).astype(BF16)
            out_ref[d] = solve(reduced, inv_ref, d)


POOL = "yl"
GATHER = ("zh", "zl")
VMEM = pltpu.VMEM


def vm(x):
    return pltpu.with_memory_space_constraint(x, pltpu.VMEM)


def call(kernel, outs, *args, scratch=(), hbm=(), out_hbm=()):
    spaces = [
        pltpu.SMEM if a.ndim == 1 else pltpu.HBM if i in hbm else pltpu.VMEM
        for i, a in enumerate(args)
    ]
    args = [
        pltpu.with_memory_space_constraint(a, pltpu.HBM) if i in hbm else a
        for i, a in enumerate(args)
    ]
    return pl.pallas_call(
        kernel,
        out_shape=outs,
        in_specs=[pl.BlockSpec(memory_space=space) for space in spaces],
        out_specs=[
            pl.BlockSpec(memory_space=pltpu.HBM if i in out_hbm else pltpu.VMEM)
            for i in range(len(outs))
        ],
        scratch_shapes=scratch,
        compiler_params=pltpu.CompilerParams(vmem_limit_bytes=16 << 20),
    )(*args)


def per_device(rhs, inverse, rhs_face, cells, weights, group_map, slab):
    subs, species, blocks, width = rhs.shape
    rows = rhs_face.shape[1]
    slots = rows // 2
    peers = lax.axis_size(SUB)
    levels = lax.axis_size(GATHER)
    slab_rows = slab.shape[0]
    own = lax.axis_index(SUB).astype(I32).reshape(1)
    side = lax.axis_index(POOL).astype(I32).reshape(1)
    rhs2 = rhs.reshape(subs, species * blocks, width)
    pairs = VMEM((subs // 2, species * blocks, 128), F32)

    half = levels * slots
    outgoing, place, whi, wlo, mapped, mine, away = call(
        front_kernel,
        [
            VMEM((peers, 4, 128), F32),
            VMEM((1, rows), F32),
            VMEM((blocks * width, rows), BF16),
            VMEM((blocks * width, rows), BF16),
            VMEM(group_map.shape, I32),
            VMEM((slab_rows, half), F32),
            pltpu.HBM((slab_rows, half), F32),
        ],
        own, side, group_map, cells, weights, rhs_face, rhs2, inverse, slab,
        scratch=[
            pairs,
            VMEM((rows, rows), BF16),
            VMEM((slab_rows, half), F32),
            VMEM(cells.shape, I32),
            VMEM(weights.shape, F32),
            VMEM(rhs_face.shape, F32),
            VMEM(rhs2.shape, BF16),
            VMEM(inverse.shape, BF16),
            pltpu.SemaphoreType.DMA((7,)),
            pltpu.SemaphoreType.DMA((2, levels)),
        ],
        hbm=range(2, 9),
        out_hbm=(6,),
    )
    incoming = lax.all_to_all(outgoing, SUB, 0, 0)
    other = lax.ppermute(away, POOL, [(0, 1), (1, 0)])
    (landing,) = call(
        landing_kernel, [VMEM((rows, slots), BF16)], own, vm(mapped),
        scratch=[VMEM((peers, rows), I32), VMEM((rows, 1), F32)],
    )
    (panel,) = call(assemble_kernel, [VMEM((species, slots), F32)], vm(incoming), vm(landing))
    panels = lax.all_to_all(jnp.broadcast_to(panel[None], (levels, species, slots)), GATHER, 0, 0)
    (partial,) = call(
        product_kernel, [VMEM((2 * peers, 8, 128), F32)],
        side, vm(panels), vm(mine), vm(other), vm(panel), vm(landing),
    )
    shares = lax.all_to_all(partial, (POOL,) + SUB, 0, 0)
    update, residual = call(
        back_kernel,
        [
            jax.ShapeDtypeStruct((subs, species * blocks, width), F32),
            jax.ShapeDtypeStruct((slab_rows // peers, species), F32),
        ],
        side, vm(shares), vm(panel), vm(place), vm(whi), vm(wlo), rhs2, inverse,
        scratch=[
            pairs,
            VMEM((rows, rows), BF16),
        ],
    )
    return update.reshape(rhs.shape), residual.T


def solution(mesh):
    fine = Mesh(mesh.devices.reshape(8, 2, 2, 4, 2, 2), ("zh", "zl", "yl", "x", "yh", "c"))
    blk, sub = ("zh", "zl", "yl"), SUB
    every = blk + sub
    placed = (
        P(every, None, None, None),
        P(every, None, None, None),
        P(None, every),
        P(None, every),
        P(None, every),
        P(blk, None),
        P(blk, sub),
    )

    return jax.shard_map(
        per_device,
        mesh=fine,
        in_specs=placed,
        out_specs=(P(every, None, None, None), P(None, every)),
        check_vma=False,
    )
```

```python
import jax
import jax.numpy as jnp
from jax import lax
from jax.experimental import pallas as pl
from jax.experimental.pallas import tpu as pltpu
from jax.sharding import Mesh
from jax.sharding import PartitionSpec as P

F32, BF16, I32 = jnp.float32, jnp.bfloat16, jnp.int32
NN = (((1,), (0,)), ((), ()))
NT = (((1,), (1,)), ((), ()))
SUB = ("x", "yh", "c")


def mxu(a, b, dims=NN):
    return lax.dot_general(a, b, dims, preferred_element_type=F32)


def halves(x):
    hi = x.astype(BF16)
    return hi, (x - hi.astype(F32)).astype(BF16)


def thirds(x):
    hi = x.astype(BF16)
    rest = x - hi.astype(F32)
    mid = rest.astype(BF16)
    return hi, mid, (rest - mid.astype(F32)).astype(BF16)


def iota(shape, axis):
    return lax.broadcasted_iota(I32, shape, axis)


def select_rows(x, onehot, dims):
    n = x.shape[0]
    y = mxu(jnp.concatenate(thirds(x), axis=0), onehot, dims)
    return y[:n] + y[n : 2 * n] + y[2 * n :]


def ranks(hit):
    n, rows = hit.shape
    hit = hit.astype(F32).astype(BF16)
    tiles = [hit[:, t : t + 128] for t in range(0, rows, 128)]
    row, col = iota((128, 256), 0), iota((128, 256), 1)
    ahead = ((row < col) | (col >= 128)).astype(F32).astype(BF16)
    counts = mxu(jnp.concatenate(tiles, axis=0), ahead)
    out, base = [], jnp.zeros((n, 128), F32)
    for t in range(len(tiles)):
        part = counts[t * n : (t + 1) * n]
        out.append(part[:, :128] + base)
        base = base + part[:, 128:]
    return jnp.concatenate(out, axis=1)


def row_numbers():
    return iota((256, 128), 0).astype(F32).astype(BF16)


def pack(x, store):
    lane = iota((4, 128), 1) // 32
    for u in range(x.shape[1] // 128):
        tile = x[:, u * 128 : (u + 1) * 128]
        turned = [tile] + [pltpu.roll(tile, k * 32, 1) for k in range(1, 4)]
        for v in range(4):
            block = turned[(0 - v) % 4][0:4]
            for b in range(1, 4):
                block = jnp.where(lane == b, turned[(b - v) % 4][4 * b : 4 * b + 4], block)
            store(4 * u + v, block)


def unpack(load, peers):
    lane = iota((4, 128), 1) // 32
    tiles = []
    for u in range(peers // 4):
        blocks = [load(4 * u + v) for v in range(4)]
        turned = [[blk] + [pltpu.roll(blk, k * 32, 1) for k in range(1, 4)] for blk in blocks]
        rows = []
        for b in range(4):
            part = turned[0][(0 - b) % 4]
            for v in range(1, 4):
                part = jnp.where(lane == v, turned[v][(v - b) % 4], part)
            rows.append(part)
        tiles.append(jnp.concatenate(rows, axis=0))
    return jnp.concatenate(tiles, axis=1)


def send_place(mapped, peers, slots):
    rows = mapped.shape[1]
    target = mapped // slots
    hit = iota((peers, rows), 0) == target
    rank = jnp.sum(jnp.where(hit, ranks(hit), 0.0), axis=0, keepdims=True)
    return target.astype(F32) * (rows // peers) + rank


def send_order(place, number, store):
    rows = place.shape[1]
    one, zero = jnp.ones((), BF16), jnp.zeros((), BF16)
    for h in range(0, rows, 256):
        inside = (place >= h) & (place < h + 256)
        local = jnp.where(inside, place - h, -1.0).astype(BF16)
        for t in range(0, rows, 128):
            store(h, t, jnp.where(number == local[:, t : t + 128], one, zero))


def coupling(cells, weights, number, store):
    coupled, rows = cells.shape
    cell = [cells[c : c + 1, :].astype(F32) for c in range(coupled)]
    weight = [weights[c : c + 1, :] for c in range(coupled)]
    for c in range(1, coupled):
        for e in range(c):
            same = cell[c] == cell[e]
            weight[e] = weight[e] + jnp.where(same, weight[c], 0.0)
            cell[c] = jnp.where(same, -1.0, cell[c])
    cell = [x.astype(BF16) for x in cell]
    parts = [halves(x) for x in weight]
    for t in range(0, rows, 128):
        high = low = jnp.zeros((256, 128), BF16)
        for c in range(coupled):
            here = number == cell[c][:, t : t + 128]
            high = jnp.where(here, parts[c][0][:, t : t + 128], high)
            low = jnp.where(here, parts[c][1][:, t : t + 128], low)
        store(t, high, low)


def solve(x, inv_ref, d):
    odd = iota((x.shape[0], 128), 0) % 2 == 1
    return jnp.where(odd, mxu(x, inv_ref[d, 1], NT), mxu(x, inv_ref[d, 0], NT))


def front_kernel(
    own_ref, side_ref, map_hbm, cells_hbm, weights_hbm, face_hbm, rhs_hbm, inv_hbm, slab_hbm,
    out_ref, place_ref, whi_ref, wlo_ref, landing_ref, mine_ref, away_hbm,
    targets, slots_of, map_ref, sums, order_ref, away_ref, cells_ref, weights_ref, face_ref, rhs_ref, inv_ref, sems, cuts,
):
    subs, twice = rhs_ref.shape[0], rhs_ref.shape[1]
    rows = face_ref.shape[1]
    peers = out_ref.shape[0]
    slots = rows // 2
    copies = [
        pltpu.make_async_copy(source, target, sems.at[i])
        for i, (source, target) in enumerate(
            (
                (map_hbm, map_ref),
                (cells_hbm, cells_ref),
                (weights_hbm, weights_ref),
                (face_hbm, face_ref),
                (rhs_hbm, rhs_ref),
                (inv_hbm, inv_ref),
            )
        )
    ]
    for copy in copies:
        copy.start()
    side = side_ref[0]
    slices = []
    for i, (member, target) in enumerate(((1 - side, away_ref), (side, mine_ref))):
        copy = pltpu.make_async_copy(slab_hbm.at[:, :, member], target, cuts.at[i])
        copy.start()
        slices.append(copy)
    number = row_numbers()
    for copy in copies[:3]:
        copy.wait()

    def order_block(h, t, block):
        order_ref[h : h + 256, t : t + 128] = block

    def coupling_block(t, high, low):
        whi_ref[:, t : t + 128] = high
        wlo_ref[:, t : t + 128] = low

    mapped = map_ref[:, pl.ds(pl.multiple_of(own_ref[0] * rows, 128), rows)]
    place = send_place(mapped, peers, slots)
    place_ref[...] = place
    send_order(place, number, order_block)
    for copy in slices[::2]:
        copy.wait()
    leaving = pltpu.make_async_copy(away_ref, away_hbm, sems.at[6])
    leaving.start()
    coupling(cells_ref[...], weights_ref[...], number, coupling_block)
    for copy in copies[3:]:
        copy.wait()
    odd = iota((twice, 128), 0) % 2 == 1
    lane = iota((twice, 128), 1)
    for t in range(subs // 2):
        parts = []
        for d in (2 * t, 2 * t + 1):
            y = solve(rhs_ref[d], inv_ref, d)
            parts.append(
                jnp.concatenate([jnp.where(odd, 0.0, y), jnp.where(odd, y, 0.0)], axis=1)
            )
        hi, lo = halves(jnp.concatenate(parts, axis=0))
        cols = slice(t * 128, (t + 1) * 128)
        z = mxu(jnp.concatenate([hi, lo], axis=0), whi_ref[:, cols])
        z = z[: 2 * twice] + z[2 * twice :] + mxu(hi, wlo_ref[:, cols])
        sums[t] = jnp.where(lane < 64, z[:twice], z[twice:])
    half = twice // 2
    faces = [
        face_ref[:, t * 128 : (t + 1) * 128]
        - (sums[t, pl.ds(0, half, stride=2), :] + sums[t, pl.ds(1, half, stride=2), :])
        for t in range(subs // 2)
    ]
    outgoing = select_rows(jnp.concatenate(faces, axis=1), order_ref[...], NT)

    def store(t, block):
        out_ref[t] = block

    pack(outgoing, store)
    landing_of(own_ref[0], map_ref, landing_ref, targets, slots_of)
    leaving.wait()
    slices[1].wait()


def landing_of(own, map_ref, out_ref, targets, slots_of):
    peers = targets.shape[0]
    rows, slots = out_ref.shape
    for p in range(peers):
        targets[p : p + 1, :] = map_ref[:, p * rows : (p + 1) * rows]
    hit = targets[...] // slots == own
    key = jnp.where(hit, ranks(hit).astype(I32), -1)
    slot = (targets[...] % slots).astype(F32)
    per = rows // peers
    for p in range(peers):
        mine = iota((per, rows), 0) == key[p : p + 1, :]
        slots_of[p * per : (p + 1) * per, :] = jnp.sum(
            jnp.where(mine, slot[p : p + 1, :], 0.0), axis=1, keepdims=True
        )
    column = slots_of[...].astype(I32)
    out_ref[...] = (iota((rows, slots), 1) == column).astype(F32).astype(BF16)


def assemble_kernel(in_ref, landing_ref, out_ref):
    incoming = unpack(lambda t: in_ref[t], in_ref.shape[0])
    out_ref[...] = select_rows(incoming, landing_ref[...], NN)


def product_kernel(
    side_ref, panels_ref, mine_ref, other_ref, panel_ref, landing_ref, out_ref
):
    count, species, slots = panels_ref.shape
    rows = mine_ref.shape[0] * 8
    peers = out_ref.shape[0] // 2
    side = side_ref[0]
    total = jnp.zeros((2 * rows, 2 * species), F32)
    low = jnp.zeros((2 * rows, species), F32)
    for j in range(count):
        tiles = [
            jnp.concatenate([ref[:, j, k].reshape(rows, 128) for ref in (mine_ref, other_ref)], axis=0)
            for k in range(slots // 128)
        ]
        shi, slo = halves(jnp.concatenate(tiles, axis=1))
        phi, plo = halves(panels_ref[j])
        total += mxu(shi, jnp.concatenate([phi, plo], axis=0), NT)
        low += mxu(slo, phi, NT)
    result = total[:, :species] + total[:, species:] + low
    result = jnp.concatenate([result, jnp.zeros((2 * rows, 128 - species), F32)], axis=1)
    mine, other = side * peers, (1 - side) * peers
    per = rows // peers
    nothing = jnp.zeros((4, 128), F32)
    for p in range(peers):
        out_ref[mine + p, 0:per, :] = result[p * per : (p + 1) * per]
        out_ref[other + p, 0:per, :] = result[rows + p * per : rows + (p + 1) * per]
        out_ref[other + p, per : per + 4, :] = nothing

    def store(t, block):
        out_ref[mine + t, per : per + 4, :] = block

    pack(select_rows(panel_ref[...], landing_ref[...], NT), store)


def back_kernel(
    side_ref, in_ref, panel_ref, place_ref, whi_ref, wlo_ref, rhs_ref, inv_ref,
    out_ref, residual_ref, twofold, order_ref,
):
    subs, twice = rhs_ref.shape[0], rhs_ref.shape[1]
    peers = in_ref.shape[0] // 2
    per, species = residual_ref.shape
    total = jnp.sum(in_ref[...], axis=0)
    eye = (iota((8, 128), 0) == iota((8, 128), 1)).astype(F32)
    first = lax.dot_general(
        eye, panel_ref[:, :128], NT, precision=lax.Precision.HIGHEST, preferred_element_type=F32
    )
    residual_ref[...] = (first - total[:, :species])[:per]
    mine = side_ref[0] * peers
    returned = unpack(lambda t: in_ref[mine + t, per : per + 4, :], peers)

    def order_block(h, t, block):
        order_ref[h : h + 256, t : t + 128] = block

    send_order(place_ref[...], row_numbers(), order_block)
    values = select_rows(returned, order_ref[...], NN)
    half = twice // 2
    for t in range(subs // 2):
        twofold[t, pl.ds(0, half, stride=2), :] = values[:, t * 128 : (t + 1) * 128]
        twofold[t, pl.ds(1, half, stride=2), :] = values[:, t * 128 : (t + 1) * 128]
    odd = iota((twice, 128), 0) % 2 == 1
    lane = iota((twice, 128), 1)
    for t in range(subs // 2):
        cols = slice(t * 128, (t + 1) * 128)
        v = twofold[t]
        hi, lo = halves(
            jnp.concatenate([jnp.where(lane < 64, v, 0.0), jnp.where(lane < 64, 0.0, v)], axis=0)
        )
        z = mxu(jnp.concatenate([hi, lo], axis=0), whi_ref[:, cols], NT)
        z = z[: 2 * twice] + z[2 * twice :] + mxu(hi, wlo_ref[:, cols], NT)
        for i, d in enumerate((2 * t, 2 * t + 1)):
            part = z[i * twice : (i + 1) * twice]
            correction = jnp.where(odd, part[:, 128:], part[:, :128])
            reduced = (rhs_ref[d].astype(F32) - correction).astype(BF16)
            out_ref[d] = solve(reduced, inv_ref, d)


POOL = "yl"
GATHER = ("zh", "zl")
VMEM = pltpu.VMEM


def vm(x):
    return pltpu.with_memory_space_constraint(x, pltpu.VMEM)


def call(kernel, outs, *args, scratch=(), hbm=(), out_hbm=()):
    spaces = [
        pltpu.SMEM if a.ndim == 1 else pltpu.HBM if i in hbm else pltpu.VMEM
        for i, a in enumerate(args)
    ]
    args = [
        pltpu.with_memory_space_constraint(a, pltpu.HBM) if i in hbm else a
        for i, a in enumerate(args)
    ]
    return pl.pallas_call(
        kernel,
        out_shape=outs,
        in_specs=[pl.BlockSpec(memory_space=space) for space in spaces],
        out_specs=[
            pl.BlockSpec(memory_space=pltpu.HBM if i in out_hbm else pltpu.VMEM)
            for i in range(len(outs))
        ],
        scratch_shapes=scratch,
        compiler_params=pltpu.CompilerParams(vmem_limit_bytes=16 << 20),
    )(*args)


def per_device(rhs, inverse, rhs_face, cells, weights, group_map, slab):
    subs, species, blocks, width = rhs.shape
    rows = rhs_face.shape[1]
    slots = rows // 2
    peers = lax.axis_size(SUB)
    levels = lax.axis_size(GATHER)
    slab_rows = slab.shape[0]
    own = lax.axis_index(SUB).astype(I32).reshape(1)
    side = lax.axis_index(POOL).astype(I32).reshape(1)
    rhs2 = rhs.reshape(subs, species * blocks, width)
    pairs = VMEM((subs // 2, species * blocks, 128), F32)

    half = (slab_rows // 8, levels, slots // 128, 8, 128)
    tiled = slab.reshape(slab_rows // 8, 8, 2 * levels * slots // 128, 128)
    tiled = jnp.transpose(tiled, (0, 2, 1, 3)).reshape(half[:2] + (2,) + half[2:])
    outgoing, place, whi, wlo, landing, mine, away = call(
        front_kernel,
        [
            VMEM((peers, 4, 128), F32),
            VMEM((1, rows), F32),
            VMEM((blocks * width, rows), BF16),
            VMEM((blocks * width, rows), BF16),
            VMEM((rows, slots), BF16),
            VMEM(half, F32),
            pltpu.HBM(half, F32),
        ],
        own, side, group_map, cells, weights, rhs_face, rhs2, inverse, tiled,
        scratch=[
            VMEM((peers, rows), I32),
            VMEM((rows, 1), F32),
            VMEM(group_map.shape, I32),
            pairs,
            VMEM((rows, rows), BF16),
            VMEM(half, F32),
            VMEM(cells.shape, I32),
            VMEM(weights.shape, F32),
            VMEM(rhs_face.shape, F32),
            VMEM(rhs2.shape, BF16),
            VMEM(inverse.shape, BF16),
            pltpu.SemaphoreType.DMA((7,)),
            pltpu.SemaphoreType.DMA((2,)),
        ],
        hbm=range(2, 9),
        out_hbm=(6,),
    )
    incoming = lax.all_to_all(outgoing, SUB, 0, 0)
    other = lax.ppermute(away, POOL, [(0, 1), (1, 0)])
    (panel,) = call(assemble_kernel, [VMEM((species, slots), F32)], vm(incoming), vm(landing))
    panels = lax.all_to_all(jnp.broadcast_to(panel[None], (levels, species, slots)), GATHER, 0, 0)
    (partial,) = call(
        product_kernel, [VMEM((2 * peers, 8, 128), F32)],
        side, vm(panels), vm(mine), vm(other), vm(panel), vm(landing),
    )
    shares = lax.all_to_all(partial, (POOL,) + SUB, 0, 0)
    update, residual = call(
        back_kernel,
        [
            jax.ShapeDtypeStruct((subs, species * blocks, width), F32),
            jax.ShapeDtypeStruct((slab_rows // peers, species), F32),
        ],
        side, vm(shares), vm(panel), vm(place), vm(whi), vm(wlo), rhs2, inverse,
        scratch=[
            pairs,
            VMEM((rows, rows), BF16),
        ],
    )
    return update.reshape(rhs.shape), residual.T


def solution(mesh):
    fine = Mesh(mesh.devices.reshape(8, 2, 2, 4, 2, 2), ("zh", "zl", "yl", "x", "yh", "c"))
    blk, sub = ("zh", "zl", "yl"), SUB
    every = blk + sub
    placed = (
        P(every, None, None, None),
        P(every, None, None, None),
        P(None, every),
        P(None, every),
        P(None, every),
        P(blk, None),
        P(blk, sub),
    )

    return jax.shard_map(
        per_device,
        mesh=fine,
        in_specs=placed,
        out_specs=(P(every, None, None, None), P(None, every)),
        check_vma=False,
    )
```

```python
import jax
import jax.numpy as jnp
from jax import lax
from jax.experimental import pallas as pl
from jax.experimental.pallas import tpu as pltpu
from jax.sharding import Mesh
from jax.sharding import PartitionSpec as P

F32, BF16, I32 = jnp.float32, jnp.bfloat16, jnp.int32
NN = (((1,), (0,)), ((), ()))
NT = (((1,), (1,)), ((), ()))
SUB = ("x", "yh", "c")


def mxu(a, b, dims=NN):
    return lax.dot_general(a, b, dims, preferred_element_type=F32)


def halves(x):
    hi = x.astype(BF16)
    return hi, (x - hi.astype(F32)).astype(BF16)


def thirds(x):
    hi = x.astype(BF16)
    rest = x - hi.astype(F32)
    mid = rest.astype(BF16)
    return hi, mid, (rest - mid.astype(F32)).astype(BF16)


def iota(shape, axis):
    return lax.broadcasted_iota(I32, shape, axis)


def select_rows(x, onehot, dims):
    n = x.shape[0]
    y = mxu(jnp.concatenate(thirds(x), axis=0), onehot, dims)
    return y[:n] + y[n : 2 * n] + y[2 * n :]


def ranks(hit):
    n, rows = hit.shape
    hit = hit.astype(F32).astype(BF16)
    tiles = [hit[:, t : t + 128] for t in range(0, rows, 128)]
    row, col = iota((128, 256), 0), iota((128, 256), 1)
    ahead = ((row < col) | (col >= 128)).astype(F32).astype(BF16)
    counts = mxu(jnp.concatenate(tiles, axis=0), ahead)
    out, base = [], jnp.zeros((n, 128), F32)
    for t in range(len(tiles)):
        part = counts[t * n : (t + 1) * n]
        out.append(part[:, :128] + base)
        base = base + part[:, 128:]
    return jnp.concatenate(out, axis=1)


def row_numbers():
    return iota((256, 128), 0).astype(F32).astype(BF16)


def pack(x, store):
    lane = iota((4, 128), 1) // 32
    for u in range(x.shape[1] // 128):
        tile = x[:, u * 128 : (u + 1) * 128]
        turned = [tile] + [pltpu.roll(tile, k * 32, 1) for k in range(1, 4)]
        for v in range(4):
            block = turned[(0 - v) % 4][0:4]
            for b in range(1, 4):
                block = jnp.where(lane == b, turned[(b - v) % 4][4 * b : 4 * b + 4], block)
            store(4 * u + v, block)


def unpack(load, peers):
    lane = iota((4, 128), 1) // 32
    tiles = []
    for u in range(peers // 4):
        blocks = [load(4 * u + v) for v in range(4)]
        turned = [[blk] + [pltpu.roll(blk, k * 32, 1) for k in range(1, 4)] for blk in blocks]
        rows = []
        for b in range(4):
            part = turned[0][(0 - b) % 4]
            for v in range(1, 4):
                part = jnp.where(lane == v, turned[v][(v - b) % 4], part)
            rows.append(part)
        tiles.append(jnp.concatenate(rows, axis=0))
    return jnp.concatenate(tiles, axis=1)


def send_place(mapped, peers, slots):
    rows = mapped.shape[1]
    target = mapped // slots
    hit = iota((peers, rows), 0) == target
    rank = jnp.sum(jnp.where(hit, ranks(hit), 0.0), axis=0, keepdims=True)
    return target.astype(F32) * (rows // peers) + rank


def send_order(place, number, store):
    rows = place.shape[1]
    one, zero = jnp.ones((), BF16), jnp.zeros((), BF16)
    for h in range(0, rows, 256):
        inside = (place >= h) & (place < h + 256)
        local = jnp.where(inside, place - h, -1.0).astype(BF16)
        for t in range(0, rows, 128):
            store(h, t, jnp.where(number == local[:, t : t + 128], one, zero))


def coupling(cells, weights, number, store):
    coupled, rows = cells.shape
    cell = [cells[c : c + 1, :].astype(F32) for c in range(coupled)]
    weight = [weights[c : c + 1, :] for c in range(coupled)]
    for c in range(1, coupled):
        for e in range(c):
            same = cell[c] == cell[e]
            weight[e] = weight[e] + jnp.where(same, weight[c], 0.0)
            cell[c] = jnp.where(same, -1.0, cell[c])
    cell = [x.astype(BF16) for x in cell]
    parts = [halves(x) for x in weight]
    for t in range(0, rows, 128):
        high = low = jnp.zeros((256, 128), BF16)
        for c in range(coupled):
            here = number == cell[c][:, t : t + 128]
            high = jnp.where(here, parts[c][0][:, t : t + 128], high)
            low = jnp.where(here, parts[c][1][:, t : t + 128], low)
        store(t, high, low)


def solve(x, inv_ref, d):
    odd = iota((x.shape[0], 128), 0) % 2 == 1
    return jnp.where(odd, mxu(x, inv_ref[d, 1], NT), mxu(x, inv_ref[d, 0], NT))


def front_kernel(
    own_ref, side_ref, map_hbm, cells_hbm, weights_hbm, face_hbm, rhs_hbm, inv_hbm, slab_hbm,
    out_ref, place_ref, whi_ref, wlo_ref, landing_ref, mine_ref, away_hbm,
    targets, slots_of, map_ref, sums, order_ref, away_ref, cells_ref, weights_ref, face_ref, rhs_ref, inv_ref, sems, cuts,
):
    subs, twice = rhs_ref.shape[0], rhs_ref.shape[1]
    rows = face_ref.shape[1]
    peers = out_ref.shape[0]
    slots = rows // 2
    copies = [
        pltpu.make_async_copy(source, target, sems.at[i])
        for i, (source, target) in enumerate(
            (
                (map_hbm, map_ref),
                (cells_hbm, cells_ref),
                (weights_hbm, weights_ref),
                (face_hbm, face_ref),
                (rhs_hbm, rhs_ref),
                (inv_hbm, inv_ref),
            )
        )
    ]
    for copy in copies:
        copy.start()
    side = side_ref[0]
    slices = []
    for i, (member, target) in enumerate(((1 - side, away_ref), (side, mine_ref))):
        copy = pltpu.make_async_copy(slab_hbm.at[:, :, member], target, cuts.at[i])
        copy.start()
        slices.append(copy)
    number = row_numbers()
    for copy in copies[:3]:
        copy.wait()

    def order_block(h, t, block):
        order_ref[h : h + 256, t : t + 128] = block

    def coupling_block(t, high, low):
        whi_ref[:, t : t + 128] = high
        wlo_ref[:, t : t + 128] = low

    mapped = map_ref[:, pl.ds(pl.multiple_of(own_ref[0] * rows, 128), rows)]
    place = send_place(mapped, peers, slots)
    place_ref[...] = place
    send_order(place, number, order_block)
    for copy in slices[::2]:
        copy.wait()
    leaving = pltpu.make_async_copy(away_ref, away_hbm, sems.at[6])
    leaving.start()
    coupling(cells_ref[...], weights_ref[...], number, coupling_block)
    for copy in copies[3:]:
        copy.wait()
    odd = iota((twice, 128), 0) % 2 == 1
    lane = iota((twice, 128), 1)
    for t in range(subs // 2):
        parts = []
        for d in (2 * t, 2 * t + 1):
            y = solve(rhs_ref[d], inv_ref, d)
            parts.append(
                jnp.concatenate([jnp.where(odd, 0.0, y), jnp.where(odd, y, 0.0)], axis=1)
            )
        hi, lo = halves(jnp.concatenate(parts, axis=0))
        cols = slice(t * 128, (t + 1) * 128)
        z = mxu(jnp.concatenate([hi, lo], axis=0), whi_ref[:, cols])
        z = z[: 2 * twice] + z[2 * twice :] + mxu(hi, wlo_ref[:, cols])
        sums[t] = jnp.where(lane < 64, z[:twice], z[twice:])
    half = twice // 2
    faces = [
        face_ref[:, t * 128 : (t + 1) * 128]
        - (sums[t, pl.ds(0, half, stride=2), :] + sums[t, pl.ds(1, half, stride=2), :])
        for t in range(subs // 2)
    ]
    outgoing = select_rows(jnp.concatenate(faces, axis=1), order_ref[...], NT)

    def store(t, block):
        out_ref[position(t, FIRST)] = block

    pack(outgoing, store)
    landing_of(own_ref[0], map_ref, landing_ref, targets, slots_of)
    leaving.wait()
    slices[1].wait()


def landing_of(own, map_ref, out_ref, targets, slots_of):
    peers = targets.shape[0]
    rows, slots = out_ref.shape
    for p in range(peers):
        targets[p : p + 1, :] = map_ref[:, p * rows : (p + 1) * rows]
    hit = targets[...] // slots == own
    key = jnp.where(hit, ranks(hit).astype(I32), -1)
    slot = (targets[...] % slots).astype(F32)
    per = rows // peers
    for p in range(peers):
        mine = iota((per, rows), 0) == key[p : p + 1, :]
        slots_of[p * per : (p + 1) * per, :] = jnp.sum(
            jnp.where(mine, slot[p : p + 1, :], 0.0), axis=1, keepdims=True
        )
    column = slots_of[...].astype(I32)
    out_ref[...] = (iota((rows, slots), 1) == column).astype(F32).astype(BF16)


def assemble_kernel(in_ref, landing_ref, out_ref):
    incoming = unpack(lambda t: in_ref[position(t, FIRST)], in_ref.shape[0])
    out_ref[...] = select_rows(incoming, landing_ref[...], NN)


def product_kernel(
    side_ref, panels_ref, mine_ref, other_ref, panel_ref, landing_ref, out_ref
):
    count, species, slots = panels_ref.shape
    rows = mine_ref.shape[0] * 8
    peers = out_ref.shape[0] // 2
    side = side_ref[0]
    total = jnp.zeros((2 * rows, 2 * species), F32)
    low = jnp.zeros((2 * rows, species), F32)
    for j in range(count):
        tiles = [
            jnp.concatenate([ref[:, LEVELS[j], k].reshape(rows, 128) for ref in (mine_ref, other_ref)], axis=0)
            for k in range(slots // 128)
        ]
        shi, slo = halves(jnp.concatenate(tiles, axis=1))
        phi, plo = halves(panels_ref[j])
        total += mxu(shi, jnp.concatenate([phi, plo], axis=0), NT)
        low += mxu(slo, phi, NT)
    result = total[:, :species] + total[:, species:] + low
    result = jnp.concatenate([result, jnp.zeros((2 * rows, 128 - species), F32)], axis=1)
    per = rows // peers
    nothing = jnp.zeros((4, 128), F32)
    for p in range(peers):
        mine, other = position(p, LAST, side), position(p, LAST, 1 - side)
        out_ref[mine, 0:per, :] = result[p * per : (p + 1) * per]
        out_ref[other, 0:per, :] = result[rows + p * per : rows + (p + 1) * per]
        out_ref[other, per : per + 4, :] = nothing

    def store(t, block):
        out_ref[position(t, LAST, side), per : per + 4, :] = block

    pack(select_rows(panel_ref[...], landing_ref[...], NT), store)


def back_kernel(
    side_ref, in_ref, panel_ref, place_ref, whi_ref, wlo_ref, rhs_ref, inv_ref,
    out_ref, residual_ref, twofold, order_ref,
):
    subs, twice = rhs_ref.shape[0], rhs_ref.shape[1]
    peers = in_ref.shape[0] // 2
    per, species = residual_ref.shape
    total = jnp.sum(in_ref[...], axis=0)
    eye = (iota((8, 128), 0) == iota((8, 128), 1)).astype(F32)
    first = lax.dot_general(
        eye, panel_ref[:, :128], NT, precision=lax.Precision.HIGHEST, preferred_element_type=F32
    )
    residual_ref[...] = (first - total[:, :species])[:per]
    side = side_ref[0]
    returned = unpack(lambda t: in_ref[position(t, LAST, side), per : per + 4, :], peers)

    def order_block(h, t, block):
        order_ref[h : h + 256, t : t + 128] = block

    send_order(place_ref[...], row_numbers(), order_block)
    values = select_rows(returned, order_ref[...], NN)
    half = twice // 2
    for t in range(subs // 2):
        twofold[t, pl.ds(0, half, stride=2), :] = values[:, t * 128 : (t + 1) * 128]
        twofold[t, pl.ds(1, half, stride=2), :] = values[:, t * 128 : (t + 1) * 128]
    odd = iota((twice, 128), 0) % 2 == 1
    lane = iota((twice, 128), 1)
    for t in range(subs // 2):
        cols = slice(t * 128, (t + 1) * 128)
        v = twofold[t]
        hi, lo = halves(
            jnp.concatenate([jnp.where(lane < 64, v, 0.0), jnp.where(lane < 64, 0.0, v)], axis=0)
        )
        z = mxu(jnp.concatenate([hi, lo], axis=0), whi_ref[:, cols], NT)
        z = z[: 2 * twice] + z[2 * twice :] + mxu(hi, wlo_ref[:, cols], NT)
        for i, d in enumerate((2 * t, 2 * t + 1)):
            part = z[i * twice : (i + 1) * twice]
            correction = jnp.where(odd, part[:, 128:], part[:, :128])
            reduced = (rhs_ref[d].astype(F32) - correction).astype(BF16)
            out_ref[d] = solve(reduced, inv_ref, d)


POOL = "yl"
GATHER = "z"
LEVELS = (8, 11, 14, 1, 4, 7, 10, 13, 0, 3, 6, 9, 12, 15, 2, 5)
FIRST = (10, 11, 14, 15, 6, 7, 8, 9, 2, 12, 3, 13, 4, 5, 0, 1)
LAST = (10, 11, 26, 27, 14, 15, 30, 31, 6, 7, 22, 24, 23, 25, 28, 29, 2, 8, 3, 9, 18, 20, 19, 21, 12, 13, 4, 5, 16, 17, 0, 1)
VMEM = pltpu.VMEM


def position(t, order, side=0):
    if len(order) == 16:
        return order.index(t)
    near, far = order.index(t), order.index(16 + t)
    return near + side * (far - near)


def vm(x):
    return pltpu.with_memory_space_constraint(x, pltpu.VMEM)


def call(kernel, outs, *args, scratch=(), hbm=(), out_hbm=()):
    spaces = [
        pltpu.SMEM if a.ndim == 1 else pltpu.HBM if i in hbm else pltpu.VMEM
        for i, a in enumerate(args)
    ]
    args = [
        pltpu.with_memory_space_constraint(a, pltpu.HBM) if i in hbm else a
        for i, a in enumerate(args)
    ]
    return pl.pallas_call(
        kernel,
        out_shape=outs,
        in_specs=[pl.BlockSpec(memory_space=space) for space in spaces],
        out_specs=[
            pl.BlockSpec(memory_space=pltpu.HBM if i in out_hbm else pltpu.VMEM)
            for i in range(len(outs))
        ],
        scratch_shapes=scratch,
        compiler_params=pltpu.CompilerParams(vmem_limit_bytes=16 << 20),
    )(*args)


def per_device(rhs, inverse, rhs_face, cells, weights, group_map, slab):
    subs, species, blocks, width = rhs.shape
    rows = rhs_face.shape[1]
    slots = rows // 2
    peers = lax.axis_size(SUB)
    levels = lax.axis_size(GATHER)
    slab_rows = slab.shape[0]
    own = lax.axis_index(SUB).astype(I32).reshape(1)
    side = lax.axis_index(POOL).astype(I32).reshape(1)
    rhs2 = rhs.reshape(subs, species * blocks, width)
    pairs = VMEM((subs // 2, species * blocks, 128), F32)

    half = (slab_rows // 8, levels, slots // 128, 8, 128)
    tiled = slab.reshape(slab_rows // 8, 8, 2 * levels * slots // 128, 128)
    tiled = jnp.transpose(tiled, (0, 2, 1, 3)).reshape(half[:2] + (2,) + half[2:])
    outgoing, place, whi, wlo, landing, mine, away = call(
        front_kernel,
        [
            VMEM((peers, 4, 128), F32),
            VMEM((1, rows), F32),
            VMEM((blocks * width, rows), BF16),
            VMEM((blocks * width, rows), BF16),
            VMEM((rows, slots), BF16),
            VMEM(half, F32),
            pltpu.HBM(half, F32),
        ],
        own, side, group_map, cells, weights, rhs_face, rhs2, inverse, tiled,
        scratch=[
            VMEM((peers, rows), I32),
            VMEM((rows, 1), F32),
            VMEM(group_map.shape, I32),
            pairs,
            VMEM((rows, rows), BF16),
            VMEM(half, F32),
            VMEM(cells.shape, I32),
            VMEM(weights.shape, F32),
            VMEM(rhs_face.shape, F32),
            VMEM(rhs2.shape, BF16),
            VMEM(inverse.shape, BF16),
            pltpu.SemaphoreType.DMA((7,)),
            pltpu.SemaphoreType.DMA((2,)),
        ],
        hbm=range(2, 9),
        out_hbm=(6,),
    )
    incoming = lax.all_to_all(outgoing, SUB, 0, 0, axis_index_groups=[list(FIRST)])
    other = lax.ppermute(away, POOL, [(0, 1), (1, 0)])
    (panel,) = call(assemble_kernel, [VMEM((species, slots), F32)], vm(incoming), vm(landing))
    panels = lax.all_to_all(
        jnp.broadcast_to(panel[None], (levels, species, slots)),
        GATHER,
        0,
        0,
        axis_index_groups=[list(LEVELS)],
    )
    (partial,) = call(
        product_kernel, [VMEM((2 * peers, 8, 128), F32)],
        side, vm(panels), vm(mine), vm(other), vm(panel), vm(landing),
    )
    shares = lax.all_to_all(
        partial, (POOL,) + SUB, 0, 0, axis_index_groups=[list(LAST)]
    )
    update, residual = call(
        back_kernel,
        [
            jax.ShapeDtypeStruct((subs, species * blocks, width), F32),
            jax.ShapeDtypeStruct((slab_rows // peers, species), F32),
        ],
        side, vm(shares), vm(panel), vm(place), vm(whi), vm(wlo), rhs2, inverse,
        scratch=[
            pairs,
            VMEM((rows, rows), BF16),
        ],
    )
    return update.reshape(rhs.shape), residual.T


def solution(mesh):
    fine = Mesh(mesh.devices.reshape(16, 2, 4, 2, 2), ("z", "yl", "x", "yh", "c"))
    blk, sub = ("z", "yl"), SUB
    every = blk + sub
    placed = (
        P(every, None, None, None),
        P(every, None, None, None),
        P(None, every),
        P(None, every),
        P(None, every),
        P(blk, None),
        P(blk, sub),
    )

    return jax.shard_map(
        per_device,
        mesh=fine,
        in_specs=placed,
        out_specs=(P(every, None, None, None), P(None, every)),
        check_vma=False,
    )
```

```python
import jax
import jax.numpy as jnp
from jax import lax
from jax.experimental import pallas as pl
from jax.experimental.pallas import tpu as pltpu
from jax.sharding import Mesh
from jax.sharding import PartitionSpec as P

F32, BF16, I32 = jnp.float32, jnp.bfloat16, jnp.int32
NN = (((1,), (0,)), ((), ()))
NT = (((1,), (1,)), ((), ()))
SUB = ("x", "yh", "c")


def mxu(a, b, dims=NN):
    return lax.dot_general(a, b, dims, preferred_element_type=F32)


def halves(x):
    hi = x.astype(BF16)
    return hi, (x - hi.astype(F32)).astype(BF16)


def thirds(x):
    hi = x.astype(BF16)
    rest = x - hi.astype(F32)
    mid = rest.astype(BF16)
    return hi, mid, (rest - mid.astype(F32)).astype(BF16)


def iota(shape, axis):
    return lax.broadcasted_iota(I32, shape, axis)


def select_rows(x, onehot, dims):
    n = x.shape[0]
    y = mxu(jnp.concatenate(thirds(x), axis=0), onehot, dims)
    return y[:n] + y[n : 2 * n] + y[2 * n :]


def ranks(hit):
    n, rows = hit.shape
    hit = hit.astype(F32).astype(BF16)
    tiles = [hit[:, t : t + 128] for t in range(0, rows, 128)]
    row, col = iota((128, 256), 0), iota((128, 256), 1)
    ahead = ((row < col) | (col >= 128)).astype(F32).astype(BF16)
    counts = mxu(jnp.concatenate(tiles, axis=0), ahead)
    out, base = [], jnp.zeros((n, 128), F32)
    for t in range(len(tiles)):
        part = counts[t * n : (t + 1) * n]
        out.append(part[:, :128] + base)
        base = base + part[:, 128:]
    return jnp.concatenate(out, axis=1)


def row_numbers():
    return iota((256, 128), 0).astype(F32).astype(BF16)


def pack(x, store):
    lane = iota((4, 128), 1) // 32
    for u in range(x.shape[1] // 128):
        tile = x[:, u * 128 : (u + 1) * 128]
        turned = [tile] + [pltpu.roll(tile, k * 32, 1) for k in range(1, 4)]
        for v in range(4):
            block = turned[(0 - v) % 4][0:4]
            for b in range(1, 4):
                block = jnp.where(lane == b, turned[(b - v) % 4][4 * b : 4 * b + 4], block)
            store(4 * u + v, block)


def unpack(load, peers):
    lane = iota((4, 128), 1) // 32
    tiles = []
    for u in range(peers // 4):
        blocks = [load(4 * u + v) for v in range(4)]
        turned = [[blk] + [pltpu.roll(blk, k * 32, 1) for k in range(1, 4)] for blk in blocks]
        rows = []
        for b in range(4):
            part = turned[0][(0 - b) % 4]
            for v in range(1, 4):
                part = jnp.where(lane == v, turned[v][(v - b) % 4], part)
            rows.append(part)
        tiles.append(jnp.concatenate(rows, axis=0))
    return jnp.concatenate(tiles, axis=1)


def send_place(mapped, peers, slots):
    rows = mapped.shape[1]
    target = mapped // slots
    hit = iota((peers, rows), 0) == target
    rank = jnp.sum(jnp.where(hit, ranks(hit), 0.0), axis=0, keepdims=True)
    return target.astype(F32) * (rows // peers) + rank


def send_order(place, number, store):
    rows = place.shape[1]
    one, zero = jnp.ones((), BF16), jnp.zeros((), BF16)
    for h in range(0, rows, 256):
        inside = (place >= h) & (place < h + 256)
        local = jnp.where(inside, place - h, -1.0).astype(BF16)
        for t in range(0, rows, 128):
            store(h, t, jnp.where(number == local[:, t : t + 128], one, zero))


def coupling(cells, weights, number, store):
    coupled, rows = cells.shape
    cell = [cells[c : c + 1, :].astype(F32) for c in range(coupled)]
    weight = [weights[c : c + 1, :] for c in range(coupled)]
    for c in range(1, coupled):
        for e in range(c):
            same = cell[c] == cell[e]
            weight[e] = weight[e] + jnp.where(same, weight[c], 0.0)
            cell[c] = jnp.where(same, -1.0, cell[c])
    cell = [x.astype(BF16) for x in cell]
    parts = [halves(x) for x in weight]
    for t in range(0, rows, 128):
        high = low = jnp.zeros((256, 128), BF16)
        for c in range(coupled):
            here = number == cell[c][:, t : t + 128]
            high = jnp.where(here, parts[c][0][:, t : t + 128], high)
            low = jnp.where(here, parts[c][1][:, t : t + 128], low)
        store(t, high, low)


def solve(x, inv_ref, d):
    odd = iota((x.shape[0], 128), 0) % 2 == 1
    return jnp.where(odd, mxu(x, inv_ref[d, 1], NT), mxu(x, inv_ref[d, 0], NT))


def front_kernel(
    own_ref, side_ref, map_hbm, cells_hbm, weights_hbm, face_hbm, rhs_hbm, inv_hbm, slab_hbm,
    out_ref, place_ref, whi_ref, wlo_ref, landing_ref, mine_ref, away_hbm,
    targets, slots_of, map_ref, sums, order_ref, away_ref, cells_ref, weights_ref, face_ref, rhs_ref, inv_ref, sems, cuts,
):
    subs, twice = rhs_ref.shape[0], rhs_ref.shape[1]
    rows = face_ref.shape[1]
    peers = out_ref.shape[0]
    slots = rows // 2
    copies = [
        pltpu.make_async_copy(source, target, sems.at[i])
        for i, (source, target) in enumerate(
            (
                (map_hbm, map_ref),
                (cells_hbm, cells_ref),
                (weights_hbm, weights_ref),
                (face_hbm, face_ref),
                (rhs_hbm, rhs_ref),
                (inv_hbm, inv_ref),
            )
        )
    ]
    for copy in copies:
        copy.start()
    side = side_ref[0]
    slices = []
    for i, (member, target) in enumerate(((1 - side, away_ref), (side, mine_ref))):
        copy = pltpu.make_async_copy(slab_hbm.at[:, :, member], target, cuts.at[i])
        copy.start()
        slices.append(copy)
    number = row_numbers()
    for copy in copies[:3]:
        copy.wait()

    def order_block(h, t, block):
        order_ref[h : h + 256, t : t + 128] = block

    def coupling_block(t, high, low):
        whi_ref[:, t : t + 128] = high
        wlo_ref[:, t : t + 128] = low

    mapped = map_ref[:, pl.ds(pl.multiple_of(own_ref[0] * rows, 128), rows)]
    place = send_place(mapped, peers, slots)
    place_ref[...] = place
    send_order(place, number, order_block)
    for copy in slices[::2]:
        copy.wait()
    leaving = pltpu.make_async_copy(away_ref, away_hbm, sems.at[6])
    leaving.start()
    coupling(cells_ref[...], weights_ref[...], number, coupling_block)
    for copy in copies[3:]:
        copy.wait()
    odd = iota((twice, 128), 0) % 2 == 1
    lane = iota((twice, 128), 1)
    for t in range(subs // 2):
        parts = []
        for d in (2 * t, 2 * t + 1):
            y = solve(rhs_ref[d], inv_ref, d)
            parts.append(
                jnp.concatenate([jnp.where(odd, 0.0, y), jnp.where(odd, y, 0.0)], axis=1)
            )
        hi, lo = halves(jnp.concatenate(parts, axis=0))
        cols = slice(t * 128, (t + 1) * 128)
        z = mxu(jnp.concatenate([hi, lo], axis=0), whi_ref[:, cols])
        z = z[: 2 * twice] + z[2 * twice :] + mxu(hi, wlo_ref[:, cols])
        sums[t] = jnp.where(lane < 64, z[:twice], z[twice:])
    half = twice // 2
    faces = [
        face_ref[:, t * 128 : (t + 1) * 128]
        - (sums[t, pl.ds(0, half, stride=2), :] + sums[t, pl.ds(1, half, stride=2), :])
        for t in range(subs // 2)
    ]
    outgoing = select_rows(jnp.concatenate(faces, axis=1), order_ref[...], NT)

    def store(t, block):
        out_ref[position(t, FIRST)] = block

    pack(outgoing, store)
    landing_of(own_ref[0], map_ref, landing_ref, targets, slots_of)
    leaving.wait()
    slices[1].wait()


def landing_of(own, map_ref, out_ref, targets, slots_of):
    peers = targets.shape[0]
    rows, slots = out_ref.shape
    for p in range(peers):
        targets[p : p + 1, :] = map_ref[:, p * rows : (p + 1) * rows]
    hit = targets[...] // slots == own
    key = jnp.where(hit, ranks(hit).astype(I32), -1)
    slot = (targets[...] % slots).astype(F32)
    per = rows // peers
    for p in range(peers):
        mine = iota((per, rows), 0) == key[p : p + 1, :]
        slots_of[p * per : (p + 1) * per, :] = jnp.sum(
            jnp.where(mine, slot[p : p + 1, :], 0.0), axis=1, keepdims=True
        )
    column = slots_of[...].astype(I32)
    out_ref[...] = (iota((rows, slots), 1) == column).astype(F32).astype(BF16)


def assemble_kernel(in_ref, landing_ref, out_ref):
    incoming = unpack(lambda t: in_ref[position(t, FIRST)], in_ref.shape[0])
    out_ref[...] = select_rows(incoming, landing_ref[...], NN)


def product_kernel(
    side_ref, panels_ref, mine_ref, other_ref, panel_ref, landing_ref, out_ref
):
    count, species, slots = panels_ref.shape
    rows = mine_ref.shape[0] * 8
    peers = out_ref.shape[0] // 2
    side = side_ref[0]
    total = jnp.zeros((2 * rows, 2 * species), F32)
    low = jnp.zeros((2 * rows, species), F32)
    for j in range(count):
        tiles = [
            jnp.concatenate([ref[:, LEVELS[j], k].reshape(rows, 128) for ref in (mine_ref, other_ref)], axis=0)
            for k in range(slots // 128)
        ]
        shi, slo = halves(jnp.concatenate(tiles, axis=1))
        phi, plo = halves(panels_ref[j])
        total += mxu(shi, jnp.concatenate([phi, plo], axis=0), NT)
        low += mxu(slo, phi, NT)
    result = total[:, :species] + total[:, species:] + low
    result = jnp.concatenate([result, jnp.zeros((2 * rows, 128 - species), F32)], axis=1)
    per = rows // peers
    nothing = jnp.zeros((4, 128), F32)
    for p in range(peers):
        mine, other = position(p, LAST, side), position(p, LAST, 1 - side)
        out_ref[mine, 0:per, :] = result[p * per : (p + 1) * per]
        out_ref[other, 0:per, :] = result[rows + p * per : rows + (p + 1) * per]
        out_ref[other, per : per + 4, :] = nothing

    def store(t, block):
        out_ref[position(t, LAST, side), per : per + 4, :] = block

    pack(select_rows(panel_ref[...], landing_ref[...], NT), store)


def back_kernel(
    side_ref, in_ref, panel_ref, place_ref, whi_ref, wlo_ref, rhs_ref, inv_ref,
    out_ref, residual_ref, twofold, order_ref,
):
    subs, twice = rhs_ref.shape[0], rhs_ref.shape[1]
    peers = in_ref.shape[0] // 2
    per, species = residual_ref.shape
    total = jnp.sum(in_ref[...], axis=0)
    eye = (iota((8, 128), 0) == iota((8, 128), 1)).astype(F32)
    first = lax.dot_general(
        eye, panel_ref[:, :128], NT, precision=lax.Precision.HIGHEST, preferred_element_type=F32
    )
    residual_ref[...] = (first - total[:, :species])[:per]
    side = side_ref[0]
    returned = unpack(lambda t: in_ref[position(t, LAST, side), per : per + 4, :], peers)

    def order_block(h, t, block):
        order_ref[h : h + 256, t : t + 128] = block

    send_order(place_ref[...], row_numbers(), order_block)
    values = select_rows(returned, order_ref[...], NN)
    half = twice // 2
    for t in range(subs // 2):
        twofold[t, pl.ds(0, half, stride=2), :] = values[:, t * 128 : (t + 1) * 128]
        twofold[t, pl.ds(1, half, stride=2), :] = values[:, t * 128 : (t + 1) * 128]
    odd = iota((twice, 128), 0) % 2 == 1
    lane = iota((twice, 128), 1)
    for t in range(subs // 2):
        cols = slice(t * 128, (t + 1) * 128)
        v = twofold[t]
        hi, lo = halves(
            jnp.concatenate([jnp.where(lane < 64, v, 0.0), jnp.where(lane < 64, 0.0, v)], axis=0)
        )
        z = mxu(jnp.concatenate([hi, lo], axis=0), whi_ref[:, cols], NT)
        z = z[: 2 * twice] + z[2 * twice :] + mxu(hi, wlo_ref[:, cols], NT)
        for i, d in enumerate((2 * t, 2 * t + 1)):
            part = z[i * twice : (i + 1) * twice]
            correction = jnp.where(odd, part[:, 128:], part[:, :128])
            reduced = (rhs_ref[d].astype(F32) - correction).astype(BF16)
            out_ref[d] = solve(reduced, inv_ref, d)


POOL = "yl"
GATHER = "z"
LEVELS = (8, 5, 2, 15, 12, 9, 6, 3, 0, 13, 10, 7, 4, 1, 14, 11)
FIRST = (10, 11, 6, 7, 14, 15, 8, 9, 2, 4, 3, 5, 12, 13, 0, 1)
LAST = (10, 11, 26, 27, 6, 7, 22, 23, 14, 24, 15, 25, 30, 31, 20, 21, 2, 8, 3, 9, 18, 19, 4, 28, 5, 29, 12, 16, 13, 17, 0, 1)
VMEM = pltpu.VMEM


def position(t, order, side=0):
    if len(order) == 16:
        return order.index(t)
    near, far = order.index(t), order.index(16 + t)
    return near + side * (far - near)


def vm(x):
    return pltpu.with_memory_space_constraint(x, pltpu.VMEM)


def call(kernel, outs, *args, scratch=(), hbm=(), out_hbm=()):
    spaces = [
        pltpu.SMEM if a.ndim == 1 else pltpu.HBM if i in hbm else pltpu.VMEM
        for i, a in enumerate(args)
    ]
    args = [
        pltpu.with_memory_space_constraint(a, pltpu.HBM) if i in hbm else a
        for i, a in enumerate(args)
    ]
    return pl.pallas_call(
        kernel,
        out_shape=outs,
        in_specs=[pl.BlockSpec(memory_space=space) for space in spaces],
        out_specs=[
            pl.BlockSpec(memory_space=pltpu.HBM if i in out_hbm else pltpu.VMEM)
            for i in range(len(outs))
        ],
        scratch_shapes=scratch,
        compiler_params=pltpu.CompilerParams(vmem_limit_bytes=16 << 20),
    )(*args)


def per_device(rhs, inverse, rhs_face, cells, weights, group_map, slab):
    subs, species, blocks, width = rhs.shape
    rows = rhs_face.shape[1]
    slots = rows // 2
    peers = lax.axis_size(SUB)
    levels = lax.axis_size(GATHER)
    slab_rows = slab.shape[0]
    own = lax.axis_index(SUB).astype(I32).reshape(1)
    side = lax.axis_index(POOL).astype(I32).reshape(1)
    rhs2 = rhs.reshape(subs, species * blocks, width)
    pairs = VMEM((subs // 2, species * blocks, 128), F32)

    half = (slab_rows // 8, levels, slots // 128, 8, 128)
    tiled = slab.reshape(slab_rows // 8, 8, 2 * levels * slots // 128, 128)
    tiled = jnp.transpose(tiled, (0, 2, 1, 3)).reshape(half[:2] + (2,) + half[2:])
    outgoing, place, whi, wlo, landing, mine, away = call(
        front_kernel,
        [
            VMEM((peers, 4, 128), F32),
            VMEM((1, rows), F32),
            VMEM((blocks * width, rows), BF16),
            VMEM((blocks * width, rows), BF16),
            VMEM((rows, slots), BF16),
            VMEM(half, F32),
            pltpu.HBM(half, F32),
        ],
        own, side, group_map, cells, weights, rhs_face, rhs2, inverse, tiled,
        scratch=[
            VMEM((peers, rows), I32),
            VMEM((rows, 1), F32),
            VMEM(group_map.shape, I32),
            pairs,
            VMEM((rows, rows), BF16),
            VMEM(half, F32),
            VMEM(cells.shape, I32),
            VMEM(weights.shape, F32),
            VMEM(rhs_face.shape, F32),
            VMEM(rhs2.shape, BF16),
            VMEM(inverse.shape, BF16),
            pltpu.SemaphoreType.DMA((7,)),
            pltpu.SemaphoreType.DMA((2,)),
        ],
        hbm=range(2, 9),
        out_hbm=(6,),
    )
    incoming = lax.all_to_all(outgoing, SUB, 0, 0, axis_index_groups=[list(FIRST)])
    other = lax.ppermute(away, POOL, [(0, 1), (1, 0)])
    (panel,) = call(assemble_kernel, [VMEM((species, slots), F32)], vm(incoming), vm(landing))
    panels = lax.all_to_all(
        jnp.broadcast_to(panel[None], (levels, species, slots)),
        GATHER,
        0,
        0,
        axis_index_groups=[list(LEVELS)],
    )
    (partial,) = call(
        product_kernel, [VMEM((2 * peers, 8, 128), F32)],
        side, vm(panels), vm(mine), vm(other), vm(panel), vm(landing),
    )
    shares = lax.all_to_all(
        partial, (POOL,) + SUB, 0, 0, axis_index_groups=[list(LAST)]
    )
    update, residual = call(
        back_kernel,
        [
            jax.ShapeDtypeStruct((subs, species * blocks, width), F32),
            jax.ShapeDtypeStruct((slab_rows // peers, species), F32),
        ],
        side, vm(shares), vm(panel), vm(place), vm(whi), vm(wlo), rhs2, inverse,
        scratch=[
            pairs,
            VMEM((rows, rows), BF16),
        ],
    )
    return update.reshape(rhs.shape), residual.T


def solution(mesh):
    fine = Mesh(mesh.devices.reshape(16, 2, 4, 2, 2), ("z", "yl", "x", "yh", "c"))
    blk, sub = ("z", "yl"), SUB
    every = blk + sub
    placed = (
        P(every, None, None, None),
        P(every, None, None, None),
        P(None, every),
        P(None, every),
        P(None, every),
        P(blk, None),
        P(blk, sub),
    )

    return jax.shard_map(
        per_device,
        mesh=fine,
        in_specs=placed,
        out_specs=(P(every, None, None, None), P(None, every)),
        check_vma=False,
    )
```
